128 devices in a mesh: band: 64 (over y, x, z), mp: 2 (over core).
Axes of the slice: x: 4, y: 4, z: 4, core: 2. Of those that a mesh axis runs over, the one named last changes fastest.
Arguments:
- grid_nodes: bfloat16 [262144, 512], P('band', 'mp'), may hold values from -6 to 6
- mesh_nodes: bfloat16 [32768, 512], P('band', 'mp'), may hold values from -6 to 6
- send_weight: bfloat16 [512, 512], P(None, 'mp'), may hold values from -0.25 to 0.25
- self_weight: bfloat16 [512, 512], P(None, 'mp'), may hold values from -0.25 to 0.25
- pooled_weight: bfloat16 [512, 512], P(None, 'mp'), may hold values from -0.25 to 0.25
- out_weight: bfloat16 [512, 2, 512], P('mp'), may hold values from -0.25 to 0.25
- encode_source: int32 [12288], P('band'), may hold values from 0 to 31
- encode_slot: int32 [12288], P('band'), may hold values from 0 to 63
- encode_tiles: bfloat16 [12288, 128, 128], P('band'), may hold values from -0.078125 to 0.078125
- slot_block: int32 [64, 64], P('band'), may hold values from 0 to 3
- decode_slot: int32 [12288], P('band'), may hold values from 0 to 63
- decode_target: int32 [12288], P('band'), may hold values from 0 to 31
- decode_tiles: bfloat16 [12288, 128, 128], P('band'), may hold values from -0.21875 to 0.21875
Outputs:
- grid_state: bfloat16 [262144, 512], P('band', 'mp')
- mesh_state: bfloat16 [32768, 512], P('band', 'mp')
The draws below stay inside these ranges and needn't reach their ends.
All inputs are finite; a program needn't handle non-finite values.
Results may differ from the reference program's by a relative error of at most 0.005.
Values may be sent and summed in bfloat16 or wider, within the bound.
No kernel may reach another device: no remote copies, remote signals or barrier semaphores. Data moves between devices by JAX's collectives and lax.ppermute only.
A program may use at most 192 MiB of HBM per device.

```python
import math
import jax
import jax.numpy as jnp
import numpy as np
from jax import lax

D = 512
HID = 512
BLOCK = 128
GB_DEV = 32
MB_DEV = 4
TPB = 6
E_ALL = 12288
GRID = 262144
MESH = 32768
N_BAND = 64


def plant(values, rng, least, largest):
    longest = values.shape.index(max(values.shape))
    spots = []
    for shift in (0, 1):
        where = [jax.random.randint(jax.random.fold_in(rng, axis), (), 0, length) for axis, length in enumerate(values.shape)]
        where[longest] = (where[longest] + shift) % values.shape[longest]
        spots.append(tuple(where))
    return values.at[spots[0]].set(least).at[spots[1]].set(largest)


def block_levels(rng, shape, cuts, least, top_value):
    gain, own = 1.0, jax.random.fold_in(rng, 6)
    for axis_at, blocks in cuts:
        heights = jnp.exp(jax.random.uniform(jax.random.fold_in(own, axis_at), (blocks,), jnp.float32, least / len(cuts), top_value / len(cuts)))
        gain = gain * jnp.repeat(heights, shape[axis_at] // blocks).reshape([-1 if axis == axis_at else 1 for axis in range(len(shape))])
    return gain


def cumulative_ranks(amount, slope):
    loads = [(1 << 20) // math.isqrt(rank ** slope) + 1 for rank in range(1, amount + 1)]
    deviation = 1 + sum(loads) // (1 << 30)
    return np.cumsum(np.array([max(1, weight // deviation) for weight in loads]))


def ranked_ids(stream_key, extent, amount, skew):
    grid = cumulative_ranks(amount, skew)
    ticket = jax.random.randint(jax.random.fold_in(stream_key, 1), extent, 0, int(grid[amount - 1]))
    standing = jnp.searchsorted(jnp.asarray(grid, jnp.int32), ticket, side="right")
    return jax.random.permutation(jax.random.fold_in(stream_key, 2), amount)[standing].astype(jnp.int32)


def bell_draw(key, extent, width, most, cuts=(), held_as=jnp.bfloat16):
    values = jax.random.normal(key, extent, jnp.float32) * width
    if len(cuts) > 0:
        values = block_levels(key, extent, cuts, -0.22, 0.18) * values
    return jnp.clip(values, min=-most, max=most).astype(held_as)


def setup_inputs(seed: int = 0) -> dict:
    seeds = jax.random.split(jax.random.key(seed), 14)
    return {
        "grid_nodes": bell_draw(seeds[0], (GRID, D), 1.0, 6.0, ((0, 64), (1, 2))),
        "mesh_nodes": bell_draw(seeds[1], (MESH, D), 1.0, 6.0, ((0, 64), (1, 2))),
        "send_weight": bell_draw(seeds[2], (D, D), D ** -0.5, 0.25, ((1, 2),)),
        "self_weight": bell_draw(seeds[3], (D, HID), D ** -0.5, 0.25, ((1, 2),)),
        "pooled_weight": bell_draw(seeds[4], (D, HID), D ** -0.5, 0.25, ((1, 2),)),
        "out_weight": bell_draw(seeds[5], (HID, 2, D), HID ** -0.5, 0.25, ((0, 2),)),
        "encode_source": plant(jax.random.randint(seeds[6], (E_ALL,), 0, GB_DEV), jax.random.fold_in(seeds[6], 1), 0, GB_DEV - 1).astype(jnp.int32),
        "encode_slot": plant(ranked_ids(seeds[7], (E_ALL,), N_BAND, 2), jax.random.fold_in(seeds[7], 3), 0, N_BAND - 1).astype(jnp.int32),
        "encode_tiles": bell_draw(seeds[8], (E_ALL, BLOCK, BLOCK), (TPB * GB_DEV * BLOCK // MB_DEV) ** -0.5, 0.078125, ((0, 64),)),
        "slot_block": plant(jax.random.randint(seeds[9], (N_BAND, N_BAND), 0, MB_DEV), jax.random.fold_in(seeds[9], 1), 0, MB_DEV - 1).astype(jnp.int32),
        "decode_slot": plant(ranked_ids(seeds[10], (E_ALL,), N_BAND, 2), jax.random.fold_in(seeds[10], 3), 0, N_BAND - 1).astype(jnp.int32),
        "decode_target": plant(jax.random.randint(seeds[11], (E_ALL,), 0, GB_DEV), jax.random.fold_in(seeds[11], 1), 0, GB_DEV - 1).astype(jnp.int32),
        "decode_tiles": bell_draw(seeds[12], (E_ALL, BLOCK, BLOCK), (TPB * BLOCK) ** -0.5, 0.21875, ((0, 64),)),
    }


def reference(grid_nodes, mesh_nodes, send_weight, self_weight, pooled_weight, out_weight, encode_source, encode_slot, encode_tiles, slot_block, decode_slot, decode_target, decode_tiles):
    tile_count = TPB * GB_DEV
    message = jax.nn.silu(jnp.dot(grid_nodes, send_weight, preferred_element_type=jnp.float32)).astype(jnp.bfloat16)
    message_blocks = message.reshape(N_BAND, GB_DEV, BLOCK, D)
    source_rows = encode_source.reshape(N_BAND, tile_count)
    slot_rows = encode_slot.reshape(N_BAND, tile_count)
    tile_rows = encode_tiles.reshape(N_BAND, tile_count, BLOCK, BLOCK)

    def encode_band(aggregate, inputs):
        band_blocks, sources, slots, tiles, linked = inputs
        picked = band_blocks[sources]
        partial_value = jnp.einsum("eij,ejc->eic", tiles.astype(jnp.float32), picked.astype(jnp.float32))
        slot_sum = jax.ops.segment_sum(partial_value, slots, num_segments=N_BAND)
        targets = jnp.arange(N_BAND, dtype=jnp.int32) * MB_DEV + linked
        return aggregate.at[targets].add(slot_sum), None

    start = jnp.zeros((N_BAND * MB_DEV, BLOCK, D), jnp.float32)
    aggregate, _ = lax.scan(encode_band, start, (message_blocks, source_rows, slot_rows, tile_rows, slot_block))
    pooled = aggregate.reshape(N_BAND * MB_DEV * BLOCK, D).astype(jnp.bfloat16)
    inner = jnp.dot(mesh_nodes, self_weight, preferred_element_type=jnp.float32) + jnp.dot(pooled, pooled_weight, preferred_element_type=jnp.float32)
    hidden = jax.nn.silu(inner).astype(jnp.bfloat16)
    projected = jnp.dot(hidden, out_weight.reshape(HID, 2 * D), preferred_element_type=jnp.float32).reshape(-1, 2, D)
    mesh_state = (mesh_nodes.astype(jnp.float32) + projected[:, 0, :]).astype(jnp.bfloat16)
    decode_source = projected[:, 1, :].astype(jnp.bfloat16).reshape(N_BAND * MB_DEV, BLOCK, D)

    def decode_band(inputs):
        slots, targets, tiles, linked, grid_band = inputs
        mesh_index = slots * MB_DEV + linked[slots]
        picked = decode_source[mesh_index]
        partial_value = jnp.einsum("eij,ejc->eic", tiles.astype(jnp.float32), picked.astype(jnp.float32))
        grid_sum = jax.ops.segment_sum(partial_value, targets, num_segments=GB_DEV)
        return (grid_band.astype(jnp.float32) + grid_sum.reshape(GB_DEV * BLOCK, D)).astype(jnp.bfloat16)

    grid_state = lax.map(decode_band, (decode_slot.reshape(N_BAND, tile_count), decode_target.reshape(N_BAND, tile_count), decode_tiles.reshape(N_BAND, tile_count, BLOCK, BLOCK), slot_block, grid_nodes.reshape(N_BAND, GB_DEV * BLOCK, D)))
    return grid_state.reshape(N_BAND * GB_DEV * BLOCK, D), mesh_state
```

```python
import functools

import jax
import jax.numpy as jnp
from jax import lax
from jax.experimental import pallas as pl
from jax.experimental.pallas import tpu as pltpu
from jax.sharding import PartitionSpec as P

MB = 1 << 20
F32 = jnp.float32
BF16 = jnp.bfloat16
SWAP = [(0, 1), (1, 0)]


def silu(v):
    return v / (1.0 + jnp.exp(-v))


def dot(a, b):
    return jnp.dot(a, b, preferred_element_type=F32)


def half(i, width):
    return pl.ds(pl.multiple_of(i * width, width), width)


def encode_body(nm, nt, slot_ref, source_ref, core_ref, own, other, weight, tiles, out, message, acc):
    step = pl.program_id(0)
    rows = own.shape[0]
    per = tiles.shape[0]
    edge = tiles.shape[1]
    per_out = out.shape[0]
    zero_step = acc.shape[0] // nm

    @pl.when(step < nm)
    def _():
        core = core_ref[0]
        k = own.shape[1]
        z = dot(own[...], weight[half(core, k), :]) + dot(other[...], weight[half(1 - core, k), :])
        value = silu(z).astype(BF16)
        blocks = rows // edge
        message[pl.ds(step * blocks, blocks)] = value.reshape(blocks, edge, value.shape[1])
        acc[pl.ds(step * zero_step, zero_step)] = jnp.zeros((zero_step, *acc.shape[1:]), F32)

    @pl.when((step >= nm) & (step < nm + nt))
    def _():
        base = (step - nm) * per
        for i in range(per):
            slot = slot_ref[base + i]
            source = source_ref[base + i]
            acc[slot] += dot(tiles[i], message[source])

    @pl.when(step >= nm + nt)
    def _():
        first = (step - nm - nt) * per_out
        out[...] = acc[pl.ds(first, per_out)].astype(BF16)


def encode(own, other, weight, tiles, source, slot, core, slots):
    rows, k = own.shape
    count, edge, _ = tiles.shape
    width = weight.shape[1]
    nm, nt, no = 8, 8, 8
    return pl.pallas_call(
        functools.partial(encode_body, nm, nt),
        out_shape=jax.ShapeDtypeStruct((slots, edge, width), BF16),
        grid_spec=pltpu.PrefetchScalarGridSpec(
            num_scalar_prefetch=3,
            grid=(nm + nt + no,),
            in_specs=[
                pl.BlockSpec((rows // nm, k), lambda i, *_: (jnp.minimum(i, nm - 1), 0)),
                pl.BlockSpec((rows // nm, k), lambda i, *_: (jnp.minimum(i, nm - 1), 0)),
                pl.BlockSpec(weight.shape, lambda i, *_: (0, 0)),
                pl.BlockSpec((count // nt, edge, edge), lambda i, *_: (jnp.clip(i - nm, 0, nt - 1), 0, 0)),
            ],
            out_specs=pl.BlockSpec((slots // no, edge, width), lambda i, *_: (jnp.clip(i - nm - nt, 0, no - 1), 0, 0)),
            scratch_shapes=[
                pltpu.VMEM((rows // edge, edge, width), BF16),
                pltpu.VMEM((slots, edge, width), F32),
            ],
        ),
        compiler_params=pltpu.CompilerParams(vmem_limit_bytes=60 * MB),
        cost_estimate=pl.CostEstimate(
            flops=2 * count * edge * edge * width, bytes_accessed=16 * MB, transcendentals=rows * width
        ),
        name="encode",
    )(slot, source, core, own, other, weight, tiles)


def mesh_body(
    nr, block_ref, link_ref, core_ref, arrived, mesh, mesh_other, self_w, self_o, pool_w, pool_o, out_w, out_o,
    keep, send, outgoing, acc, state, source,
):
    step = pl.program_id(0)
    core = core_ref[0]
    bands = arrived.shape[0] // 2
    rows, width = arrived.shape[1:]

    @pl.when(step == 0)
    def _():
        acc[...] = jnp.zeros(acc.shape, F32)

    @pl.when(step < nr)
    def _():
        for i in range(bands):
            block = block_ref[step * bands + i]
            for part in range(2):
                acc[block, :, part * width : (part + 1) * width] += arrived[2 * i + part].astype(F32)

    @pl.when(step == nr - 1)
    def _():
        pooled = acc[...].reshape(-1, 2 * width).astype(BF16)
        mine, theirs = mesh[...], mesh_other[...]
        hidden = []
        for sw, pw in ((self_w, pool_w), (self_o, pool_o)):
            inner = (
                dot(mine, sw[half(core, width), :])
                + dot(theirs, sw[half(1 - core, width), :])
                + dot(pooled, pw[...])
            )
            hidden.append(silu(inner).astype(BF16))
        full = 2 * width
        state[...] = dot(hidden[0], out_w[:, :full]) + dot(hidden[1], out_o[:, :full])
        sent = dot(hidden[0], out_w[:, full:]) + dot(hidden[1], out_o[:, full:])
        source[...] = sent.astype(BF16).reshape(source.shape)
        keep[...] = (mine.astype(F32) + state[:, half(core, width)]).astype(BF16)
        send[...] = (theirs.astype(F32) + state[:, half(1 - core, width)]).astype(BF16)

    @pl.when(step >= nr)
    def _():
        count = outgoing.shape[0] // 2
        for i in range(count):
            block = link_ref[(step - nr) * count + i]
            for part in range(2):
                outgoing[2 * i + part] = source[block, :, part * width : (part + 1) * width]


def mesh_update(arrived, owner_block, core, mesh, mesh_other, weights, blocks):
    pieces, rows, width = arrived.shape
    nr, no = 8, 8
    whole = lambda a: pl.BlockSpec(a.shape, lambda i, *_: (0,) * a.ndim)
    flat = jax.ShapeDtypeStruct(mesh.shape, BF16)
    return pl.pallas_call(
        functools.partial(mesh_body, nr),
        out_shape=(flat, flat, jax.ShapeDtypeStruct(arrived.shape, BF16)),
        grid_spec=pltpu.PrefetchScalarGridSpec(
            num_scalar_prefetch=3,
            grid=(nr + no,),
            in_specs=[
                pl.BlockSpec((pieces // nr, rows, width), lambda i, *_: (jnp.minimum(i, nr - 1), 0, 0)),
                whole(mesh),
                whole(mesh_other),
                *[whole(w) for w in weights],
            ],
            out_specs=[
                whole(flat),
                whole(flat),
                pl.BlockSpec((pieces // no, rows, width), lambda i, *_: (jnp.maximum(i - nr, 0), 0, 0)),
            ],
            scratch_shapes=[
                pltpu.VMEM((blocks, rows, 2 * width), F32),
                pltpu.VMEM((blocks * rows, 2 * width), F32),
                pltpu.VMEM((blocks, rows, 2 * width), BF16),
            ],
        ),
        compiler_params=pltpu.CompilerParams(vmem_limit_bytes=60 * MB),
        cost_estimate=pl.CostEstimate(flops=10**9, bytes_accessed=12 * MB, transcendentals=1 << 17),
        name="mesh_update",
    )(owner_block, owner_block, core, arrived, mesh, mesh_other, *weights)


def decode_body(ni, nt, slot_ref, target_ref, picked, grid_in, tiles, out, acc):
    step = pl.program_id(0)
    per = tiles.shape[0]
    per_in = grid_in.shape[0]
    per_out = out.shape[0]

    @pl.when(step < ni)
    def _():
        acc[pl.ds(step * per_in, per_in)] = grid_in[...].astype(F32)

    @pl.when((step >= ni) & (step < ni + nt))
    def _():
        base = (step - ni) * per
        for i in range(per):
            acc[target_ref[base + i]] += dot(tiles[i], picked[slot_ref[base + i]])

    @pl.when(step >= ni + nt)
    def _():
        out[...] = acc[pl.ds((step - ni - nt) * per_out, per_out)].astype(BF16)


def decode(picked, grid_blocks, tiles, slot, target):
    count, edge, _ = tiles.shape
    blocks, _, width = grid_blocks.shape
    ni, nt, no = 4, 8, 8
    return pl.pallas_call(
        functools.partial(decode_body, ni, nt),
        out_shape=jax.ShapeDtypeStruct(grid_blocks.shape, BF16),
        grid_spec=pltpu.PrefetchScalarGridSpec(
            num_scalar_prefetch=2,
            grid=(ni + nt + no,),
            in_specs=[
                pl.BlockSpec(picked.shape, lambda i, *_: (0, 0, 0)),
                pl.BlockSpec((blocks // ni, edge, width), lambda i, *_: (jnp.minimum(i, ni - 1), 0, 0)),
                pl.BlockSpec((count // nt, edge, edge), lambda i, *_: (jnp.clip(i - ni, 0, nt - 1), 0, 0)),
            ],
            out_specs=pl.BlockSpec((blocks // no, edge, width), lambda i, *_: (jnp.clip(i - ni - nt, 0, no - 1), 0, 0)),
            scratch_shapes=[pltpu.VMEM((blocks, edge, width), F32)],
        ),
        compiler_params=pltpu.CompilerParams(vmem_limit_bytes=60 * MB),
        cost_estimate=pl.CostEstimate(
            flops=2 * count * edge * edge * width, bytes_accessed=16 * MB, transcendentals=0
        ),
        name="decode",
    )(slot, target, picked, grid_blocks, tiles)


def swap(x):
    return lax.ppermute(x, "mp", SWAP)


def per_device(
    grid_nodes,
    mesh_nodes,
    send_weight,
    self_weight,
    pooled_weight,
    out_weight,
    encode_source,
    encode_slot,
    encode_tiles,
    slot_block,
    decode_slot,
    decode_target,
    decode_tiles,
):
    bands = lax.axis_size("band")
    core = lax.axis_index("mp").astype(jnp.int32)
    core_1 = core.reshape(1)
    edge = encode_tiles.shape[1]
    width = grid_nodes.shape[1]
    mesh_blocks = mesh_nodes.shape[0] // edge
    rows = edge // 2

    grid_other = swap(grid_nodes)
    owner_block = lax.all_to_all(slot_block[0], "band", split_axis=0, concat_axis=0, tiled=True)
    halves = mesh_nodes.reshape(mesh_blocks, 2, rows, width)
    mesh_keep = lax.dynamic_index_in_dim(halves, core, 1, keepdims=False).reshape(-1, width)
    mesh_send = lax.dynamic_index_in_dim(halves, 1 - core, 1, keepdims=False).reshape(-1, width)
    out_flat = out_weight.reshape(out_weight.shape[0], -1)
    mesh_other = swap(mesh_send)
    self_other, pooled_other, out_other = swap(self_weight), swap(pooled_weight), swap(out_flat)

    slot_sums = encode(
        grid_nodes, grid_other, send_weight, encode_tiles, encode_source, encode_slot, core_1, bands
    )
    arrived = lax.all_to_all(
        slot_sums.reshape(2 * bands, rows, width), ("band", "mp"), split_axis=0, concat_axis=0, tiled=True
    )
    keep, send, outgoing = mesh_update(
        arrived,
        owner_block,
        core_1,
        mesh_keep,
        mesh_other,
        (self_weight, self_other, pooled_weight, pooled_other, out_flat, out_other),
        mesh_blocks,
    )
    returned = lax.all_to_all(outgoing, ("band", "mp"), split_axis=0, concat_axis=0, tiled=True)
    came = swap(send).reshape(mesh_blocks, 1, rows, width)
    kept = keep.reshape(mesh_blocks, 1, rows, width)
    mesh_state = jnp.concatenate(
        [jnp.where(core == 0, kept, came), jnp.where(core == 0, came, kept)], axis=1
    ).reshape(mesh_nodes.shape)
    grid_state = decode(
        returned.reshape(bands, edge, width),
        grid_nodes.reshape(-1, edge, width),
        decode_tiles,
        decode_slot,
        decode_target,
    )
    return grid_state.reshape(grid_nodes.shape), mesh_state


def solution(mesh):
    return jax.shard_map(
        per_device,
        mesh=mesh,
        in_specs=(
            P("band", "mp"),
            P("band", "mp"),
            P(None, "mp"),
            P(None, "mp"),
            P(None, "mp"),
            P("mp", None, None),
            P("band"),
            P("band"),
            P("band", None, None),
            P("band", None),
            P("band"),
            P("band"),
            P("band", None, None),
        ),
        out_specs=(P("band", "mp"), P("band", "mp")),
        check_vma=False,
    )
```

```python
import functools

import jax
import jax.numpy as jnp
from jax import lax
from jax.experimental import pallas as pl
from jax.experimental.pallas import tpu as pltpu
from jax.sharding import PartitionSpec as P

MB = 1 << 20
F32 = jnp.float32
BF16 = jnp.bfloat16
SWAP = [(0, 1), (1, 0)]


def silu(v):
    return v / (1.0 + jnp.exp(-v))


def dot(a, b):
    return jnp.dot(a, b, preferred_element_type=F32)


def half(i, width):
    return pl.ds(pl.multiple_of(i * width, width), width)


def fetch(source, target, semaphores, count):
    size = source.shape[0] // count

    def piece(k):
        rows = pl.ds(k * size, size)
        return pltpu.make_async_copy(source.at[rows], target.at[rows], semaphores.at[k])

    for k in range(count):
        piece(k).start()
    return lambda k: piece(k).wait()


def hbm():
    return pl.BlockSpec(memory_space=pl.ANY)


PARAMS = pltpu.CompilerParams(vmem_limit_bytes=60 * MB)


PIECES = 4
UNROLL = 16
TAG = 8


def encode_body(
    slot_ref, source_ref, link_ref, core_ref, own_hbm, other_hbm, weight_hbm, tiles_hbm, out_hbm,
    own, other, weight, tiles, message, acc, out, own_sem, other_sem, weight_sem, tiles_sem, out_sem,
):
    core = core_ref[0]
    blocks, edge, width = message.shape
    slots = acc.shape[0]
    count = tiles.shape[0]
    rows = edge // 2
    lanes = out.shape[2]
    weight_ready = fetch(weight_hbm, weight, weight_sem, 1)
    own_ready = fetch(own_hbm, own, own_sem, PIECES)
    other_ready = fetch(other_hbm, other, other_sem, PIECES)
    tiles_ready = fetch(tiles_hbm, tiles, tiles_sem, PIECES)
    weight_ready(0)

    inner = 2 * edge
    per = blocks * edge // inner // PIECES
    cleared = slots // (per * PIECES)

    @pl.loop(0, PIECES)
    def _(piece):
        own_ready(piece)
        other_ready(piece)

        @pl.loop(0, per)
        def _(j):
            step = piece * per + j
            at = pl.ds(pl.multiple_of(step * inner, inner), inner)
            z = dot(own[at, :], weight[half(core, width), :]) + dot(other[at, :], weight[half(1 - core, width), :])
            message[pl.ds(step * 2, 2)] = silu(z).astype(BF16).reshape(2, edge, width)
            acc[pl.ds(step * cleared, cleared)] = jnp.zeros((cleared, edge, width), F32)

    @pl.loop(0, PIECES)
    def _(piece):
        tiles_ready(piece)

        @pl.loop(0, count // PIECES // UNROLL)
        def _(j):
            base = piece * (count // PIECES) + j * UNROLL
            for i in range(UNROLL):
                acc[slot_ref[base + i]] += dot(tiles[base + i], message[source_ref[base + i]])

    size = 2 * slots // PIECES

    def leave(k):
        at = pl.ds(k * size, size)
        return pltpu.make_async_copy(out.at[at], out_hbm.at[at], out_sem.at[k])

    @pl.loop(0, PIECES)
    def _(piece):
        @pl.loop(0, slots // PIECES, unroll=4)
        def _(j):
            slot = piece * (slots // PIECES) + j
            tag = jnp.full((TAG, lanes), link_ref[slot].astype(F32), F32).astype(BF16)
            for part in range(2):
                value = acc[slot, part * rows : (part + 1) * rows, :].astype(BF16)
                for column in range(2):
                    out[2 * slot + part, column * rows : (column + 1) * rows, :] = value[
                        :, column * lanes : (column + 1) * lanes
                    ]
                out[2 * slot + part, 2 * rows :, :] = tag

        leave(piece).start()

    for piece in range(PIECES):
        leave(piece).wait()


def encode(own, other, weight, tiles, source, slot, link, core, slots):
    count, edge, _ = tiles.shape
    width = weight.shape[1]
    sent = (2 * slots, edge + TAG, width // 2)
    dma = pltpu.SemaphoreType.DMA
    return pl.pallas_call(
        encode_body,
        out_shape=jax.ShapeDtypeStruct(sent, BF16),
        grid_spec=pltpu.PrefetchScalarGridSpec(
            num_scalar_prefetch=4,
            in_specs=[hbm()] * 4,
            out_specs=hbm(),
            scratch_shapes=[
                pltpu.VMEM(own.shape, BF16),
                pltpu.VMEM(other.shape, BF16),
                pltpu.VMEM(weight.shape, BF16),
                pltpu.VMEM(tiles.shape, BF16),
                pltpu.VMEM((own.shape[0] // edge, edge, width), BF16),
                pltpu.VMEM((slots, edge, width), F32),
                pltpu.VMEM(sent, BF16),
                dma((PIECES,)),
                dma((PIECES,)),
                dma((1,)),
                dma((PIECES,)),
                dma((PIECES,)),
            ],
        ),
        compiler_params=PARAMS,
        cost_estimate=pl.CostEstimate(
            flops=2 * count * edge * edge * width, bytes_accessed=16 * MB, transcendentals=own.shape[0] * width
        ),
        name="encode",
    )(slot, source, link, core, own, other, weight, tiles)


def mesh_body(core_ref, arrived_hbm, mesh_hbm, other_hbm, *refs):
    weights_hbm, refs = refs[:6], refs[6:]
    keep, send, outgoing_hbm, arrived, mine_ref, theirs_ref = refs[:6]
    weights, refs = refs[6:12], refs[12:]
    acc, state, source, outgoing, block_ref, arrived_sem, small_sem, out_sem = refs
    core = core_ref[0]
    bands = arrived.shape[0] // 2
    lanes = arrived.shape[2]
    rows = acc.shape[1]
    width = 2 * lanes
    ready = fetch(arrived_hbm, arrived, arrived_sem, PIECES)
    small = [
        pltpu.make_async_copy(x, y, small_sem.at[k])
        for k, (x, y) in enumerate(zip((mesh_hbm, other_hbm, *weights_hbm), (mine_ref, theirs_ref, *weights)))
    ]
    for copy in small:
        copy.start()
    acc[...] = jnp.zeros(acc.shape, F32)

    @pl.loop(0, PIECES)
    def _(piece):
        ready(piece)

        @pl.loop(0, bands // PIECES, unroll=4)
        def _(j):
            band = piece * (bands // PIECES) + j
            tag = arrived[2 * band, 2 * rows :, :].astype(F32)
            block = jnp.max(tag).astype(jnp.int32)
            block_ref[band] = block

        @pl.loop(0, bands // PIECES, unroll=2)
        def _(j):
            band = piece * (bands // PIECES) + j
            block = block_ref[band]
            for part in range(2):
                for column in range(2):
                    at = (2 * part + column) * lanes
                    acc[block, :, at : at + lanes] += arrived[
                        2 * band + part, column * rows : (column + 1) * rows, :
                    ].astype(F32)

    for copy in small:
        copy.wait()
    self_w, self_o, pool_w, pool_o, out_w, out_o = weights
    pooled = acc[...].reshape(-1, 2 * width).astype(BF16)
    mine, theirs = mine_ref[...], theirs_ref[...]
    hidden = []
    for sw, pw in ((self_w, pool_w), (self_o, pool_o)):
        inner = (
            dot(mine, sw[half(core, width), :]) + dot(theirs, sw[half(1 - core, width), :]) + dot(pooled, pw[...])
        )
        hidden.append(silu(inner).astype(BF16))
    full = 2 * width
    sent = dot(hidden[0], out_w[:, full:]) + dot(hidden[1], out_o[:, full:])
    source[...] = sent.astype(BF16).reshape(source.shape)

    size = 2 * bands // PIECES

    def leave(k):
        at = pl.ds(k * size, size)
        return pltpu.make_async_copy(outgoing.at[at], outgoing_hbm.at[at], out_sem.at[k])

    @pl.loop(0, PIECES)
    def _(piece):
        @pl.loop(0, bands // PIECES, unroll=4)
        def _(j):
            band = piece * (bands // PIECES) + j
            block = block_ref[band]
            for part in range(2):
                outgoing[2 * band + part] = source[block, :, part * width : (part + 1) * width]

        leave(piece).start()

    state[...] = dot(hidden[0], out_w[:, :full]) + dot(hidden[1], out_o[:, :full])
    keep[...] = (mine.astype(F32) + state[:, half(core, width)]).astype(BF16)
    send[...] = (theirs.astype(F32) + state[:, half(1 - core, width)]).astype(BF16)
    for piece in range(PIECES):
        leave(piece).wait()


def mesh_update(arrived, core, mesh, mesh_other, weights, blocks):
    pieces, height, lanes = arrived.shape
    rows, width = (height - TAG) // 2, 2 * lanes
    flat = jax.ShapeDtypeStruct(mesh.shape, BF16)
    leaving = (pieces, rows, width)
    dma = pltpu.SemaphoreType.DMA
    vmem = pl.BlockSpec(memory_space=pltpu.VMEM)
    return pl.pallas_call(
        mesh_body,
        out_shape=(flat, flat, jax.ShapeDtypeStruct(leaving, BF16)),
        grid_spec=pltpu.PrefetchScalarGridSpec(
            num_scalar_prefetch=1,
            in_specs=[hbm()] * 9,
            out_specs=[vmem, vmem, hbm()],
            scratch_shapes=[
                pltpu.VMEM(arrived.shape, BF16),
                pltpu.VMEM(mesh.shape, BF16),
                pltpu.VMEM(mesh.shape, BF16),
                *[pltpu.VMEM(w.shape, BF16) for w in weights],
                pltpu.VMEM((blocks, rows, 2 * width), F32),
                pltpu.VMEM((blocks * rows, 2 * width), F32),
                pltpu.VMEM((blocks, rows, 2 * width), BF16),
                pltpu.VMEM(leaving, BF16),
                pltpu.SMEM((pieces // 2,), jnp.int32),
                dma((PIECES,)),
                dma((8,)),
                dma((PIECES,)),
            ],
        ),
        compiler_params=PARAMS,
        cost_estimate=pl.CostEstimate(flops=10**9, bytes_accessed=12 * MB, transcendentals=1 << 17),
        name="mesh_update",
    )(core, arrived, mesh, mesh_other, *weights)


def decode_body(
    slot_ref, target_ref, picked_hbm, grid_hbm, tiles_hbm, out_hbm,
    picked, start, tiles, acc, out, picked_sem, start_sem, tiles_sem, out_sem,
):
    count = tiles.shape[0]
    blocks = acc.shape[0]
    start_ready = fetch(grid_hbm, start, start_sem, PIECES)
    picked_ready = fetch(picked_hbm, picked, picked_sem, PIECES)
    tiles_ready = fetch(tiles_hbm, tiles, tiles_sem, PIECES)
    per = blocks // PIECES

    @pl.loop(0, PIECES)
    def _(piece):
        start_ready(piece)

        @pl.loop(0, per, unroll=4)
        def _(j):
            acc[piece * per + j] = start[piece * per + j].astype(F32)

    for piece in range(PIECES):
        picked_ready(piece)

    @pl.loop(0, PIECES)
    def _(piece):
        tiles_ready(piece)

        @pl.loop(0, count // PIECES // UNROLL)
        def _(j):
            base = piece * (count // PIECES) + j * UNROLL
            for i in range(UNROLL):
                acc[target_ref[base + i]] += dot(tiles[base + i], picked[slot_ref[base + i]])

    def leave(k):
        at = pl.ds(k * per, per)
        return pltpu.make_async_copy(out.at[at], out_hbm.at[at], out_sem.at[k])

    @pl.loop(0, PIECES)
    def _(piece):
        @pl.loop(0, per, unroll=4)
        def _(j):
            out[piece * per + j] = acc[piece * per + j].astype(BF16)

        leave(piece).start()

    for piece in range(PIECES):
        leave(piece).wait()


def decode(picked, grid_blocks, tiles, slot, target):
    count, edge, _ = tiles.shape
    width = grid_blocks.shape[2]
    dma = pltpu.SemaphoreType.DMA
    return pl.pallas_call(
        decode_body,
        out_shape=jax.ShapeDtypeStruct(grid_blocks.shape, BF16),
        grid_spec=pltpu.PrefetchScalarGridSpec(
            num_scalar_prefetch=2,
            in_specs=[hbm()] * 3,
            out_specs=hbm(),
            scratch_shapes=[
                pltpu.VMEM(picked.shape, BF16),
                pltpu.VMEM(grid_blocks.shape, BF16),
                pltpu.VMEM(tiles.shape, BF16),
                pltpu.VMEM(grid_blocks.shape, F32),
                pltpu.VMEM(grid_blocks.shape, BF16),
                *[dma((PIECES,))] * 4,
            ],
        ),
        compiler_params=PARAMS,
        cost_estimate=pl.CostEstimate(
            flops=2 * count * edge * edge * width, bytes_accessed=16 * MB, transcendentals=0
        ),
        name="decode",
    )(slot, target, picked, grid_blocks, tiles)


def swap(x):
    return lax.ppermute(x, "mp", SWAP)


def per_device(
    grid_nodes,
    mesh_nodes,
    send_weight,
    self_weight,
    pooled_weight,
    out_weight,
    encode_source,
    encode_slot,
    encode_tiles,
    slot_block,
    decode_slot,
    decode_target,
    decode_tiles,
):
    bands = lax.axis_size("band")
    core = lax.axis_index("mp").astype(jnp.int32)
    core_1 = core.reshape(1)
    edge = encode_tiles.shape[1]
    width = grid_nodes.shape[1]
    mesh_blocks = mesh_nodes.shape[0] // edge
    rows = edge // 2

    grid_other = swap(grid_nodes)
    halves = mesh_nodes.reshape(mesh_blocks, 2, rows, width)
    mesh_keep = lax.dynamic_index_in_dim(halves, core, 1, keepdims=False).reshape(-1, width)
    mesh_send = lax.dynamic_index_in_dim(halves, 1 - core, 1, keepdims=False).reshape(-1, width)
    out_flat = out_weight.reshape(out_weight.shape[0], -1)
    mesh_other = swap(mesh_send)
    self_other, pooled_other, out_other = swap(self_weight), swap(pooled_weight), swap(out_flat)

    slot_sums = encode(
        grid_nodes, grid_other, send_weight, encode_tiles, encode_source, encode_slot, slot_block[0], core_1, bands
    )
    arrived = lax.all_to_all(slot_sums, ("band", "mp"), split_axis=0, concat_axis=0, tiled=True)
    keep, send, outgoing = mesh_update(
        arrived,
        core_1,
        mesh_keep,
        mesh_other,
        (self_weight, self_other, pooled_weight, pooled_other, out_flat, out_other),
        mesh_blocks,
    )
    returned = lax.all_to_all(outgoing, ("band", "mp"), split_axis=0, concat_axis=0, tiled=True)
    came = swap(send).reshape(mesh_blocks, 1, rows, width)
    kept = keep.reshape(mesh_blocks, 1, rows, width)
    mesh_state = jnp.concatenate(
        [jnp.where(core == 0, kept, came), jnp.where(core == 0, came, kept)], axis=1
    ).reshape(mesh_nodes.shape)
    grid_state = decode(
        returned.reshape(bands, edge, width),
        grid_nodes.reshape(-1, edge, width),
        decode_tiles,
        decode_slot,
        decode_target,
    )
    return grid_state.reshape(grid_nodes.shape), mesh_state


def solution(mesh):
    return jax.shard_map(
        per_device,
        mesh=mesh,
        in_specs=(
            P("band", "mp"),
            P("band", "mp"),
            P(None, "mp"),
            P(None, "mp"),
            P(None, "mp"),
            P("mp", None, None),
            P("band"),
            P("band"),
            P("band", None, None),
            P("band", None),
            P("band"),
            P("band"),
            P("band", None, None),
        ),
        out_specs=(P("band", "mp"), P("band", "mp")),
        check_vma=False,
    )
```

```python
import functools

import jax
import jax.numpy as jnp
from jax import lax
from jax.experimental import pallas as pl
from jax.experimental.pallas import tpu as pltpu
from jax.sharding import PartitionSpec as P

MB = 1 << 20
F32 = jnp.float32
BF16 = jnp.bfloat16
SWAP = [(0, 1), (1, 0)]


def silu(v):
    return v / (1.0 + jnp.exp(-v))


def dot(a, b):
    return jnp.dot(a, b, preferred_element_type=F32)


def half(i, width):
    return pl.ds(pl.multiple_of(i * width, width), width)


def fetch(source, target, semaphores, count):
    size = source.shape[0] // count

    def piece(k):
        rows = pl.ds(k * size, size)
        return pltpu.make_async_copy(source.at[rows], target.at[rows], semaphores.at[k])

    return lambda k: piece(k).start(), lambda k: piece(k).wait()


def hbm():
    return pl.BlockSpec(memory_space=pltpu.HBM)


def stay(*arrays):
    return tuple(pltpu.with_memory_space_constraint(a, pltpu.HBM) for a in arrays)


def vmem():
    return pl.BlockSpec(memory_space=pltpu.VMEM)


WIDE = pltpu.CompilerParams(vmem_limit_bytes=56 * MB)
NARROW = pltpu.CompilerParams(vmem_limit_bytes=44 * MB)


PIECES = 4
UNROLL = 48
TAG = 8


def encode_body(
    slot_ref, source_ref, link_ref, core_ref, own_hbm, other, weight, tiles_hbm, out_hbm,
    own, tiles, message, acc, out, own_sem, tiles_sem, out_sem,
):
    core = core_ref[0]
    blocks, edge, width = message.shape
    slots = acc.shape[0]
    count = tiles.shape[0]
    rows = edge // 2
    lanes = out.shape[2]
    own_start, own_ready = fetch(own_hbm, own, own_sem, PIECES)
    tiles_start, tiles_ready = fetch(tiles_hbm, tiles, tiles_sem, PIECES)
    for piece in range(PIECES):
        own_start(piece)

    inner = 8 * edge
    per = blocks * edge // inner // PIECES
    cleared = slots // (per * PIECES)

    @pl.loop(0, PIECES)
    def _(piece):
        own_ready(piece)
        tiles_start(piece)

        @pl.loop(0, per)
        def _(j):
            step = piece * per + j
            at = pl.ds(pl.multiple_of(step * inner, inner), inner)
            z = dot(own[at, :], weight[half(core, width), :]) + dot(other[at, :], weight[half(1 - core, width), :])
            message[pl.ds(step * 8, 8)] = silu(z).astype(BF16).reshape(8, edge, width)
            acc[pl.ds(step * cleared, cleared)] = jnp.zeros((cleared, edge, width), F32)

    @pl.loop(0, PIECES)
    def _(piece):
        tiles_ready(piece)

        @pl.loop(0, count // PIECES // UNROLL)
        def _(j):
            base = piece * (count // PIECES) + j * UNROLL
            for i in range(UNROLL):
                acc[slot_ref[base + i]] += dot(tiles[base + i], message[source_ref[base + i]])

    size = 2 * slots // PIECES

    def leave(k):
        at = pl.ds(k * size, size)
        return pltpu.make_async_copy(out.at[at], out_hbm.at[at], out_sem.at[k])

    @pl.loop(0, PIECES)
    def _(piece):
        @pl.loop(0, slots // PIECES, unroll=4)
        def _(j):
            slot = piece * (slots // PIECES) + j
            tag = jnp.full((TAG, lanes), link_ref[slot].astype(F32), F32).astype(BF16)
            for part in range(2):
                value = acc[slot, part * rows : (part + 1) * rows, :].astype(BF16)
                for column in range(2):
                    out[2 * slot + part, column * rows : (column + 1) * rows, :] = value[
                        :, column * lanes : (column + 1) * lanes
                    ]
                out[2 * slot + part, 2 * rows :, :] = tag

        leave(piece).start()

    for piece in range(PIECES):
        leave(piece).wait()


def encode(own, other, weight, tiles, source, slot, link, core, slots):
    count, edge, _ = tiles.shape
    width = weight.shape[1]
    sent = (2 * slots, edge + TAG, width // 2)
    dma = pltpu.SemaphoreType.DMA
    return pl.pallas_call(
        encode_body,
        out_shape=pltpu.HBM(sent, BF16),
        grid_spec=pltpu.PrefetchScalarGridSpec(
            num_scalar_prefetch=4,
            in_specs=[hbm(), vmem(), vmem(), hbm()],
            out_specs=hbm(),
            scratch_shapes=[
                pltpu.VMEM(own.shape, BF16),
                pltpu.VMEM(tiles.shape, BF16),
                pltpu.VMEM((own.shape[0] // edge, edge, width), BF16),
                pltpu.VMEM((slots, edge, width), F32),
                pltpu.VMEM(sent, BF16),
                *[dma((PIECES,))] * 3,
            ],
        ),
        compiler_params=WIDE,
        cost_estimate=pl.CostEstimate(
            flops=2 * count * edge * edge * width, bytes_accessed=16 * MB, transcendentals=own.shape[0] * width
        ),
        name="encode",
    )(slot, source, link, core, *stay(own), other, weight, *stay(tiles))


def mesh_body(
    core_ref, arrived_hbm, mine_ref, theirs_ref, self_w, self_o, pool_w, pool_o, out_w, out_o, keep, send,
    outgoing_hbm, arrived, acc, state, source, outgoing, block_ref, arrived_sem, out_sem,
):
    core = core_ref[0]
    bands = arrived.shape[0] // 2
    lanes = arrived.shape[2]
    rows = acc.shape[1]
    width = 2 * lanes
    arrived_start, ready = fetch(arrived_hbm, arrived, arrived_sem, PIECES)
    for piece in range(PIECES):
        arrived_start(piece)
    acc[...] = jnp.zeros(acc.shape, F32)

    @pl.loop(0, PIECES)
    def _(piece):
        ready(piece)

        @pl.loop(0, bands // PIECES, unroll=16)
        def _(j):
            band = piece * (bands // PIECES) + j
            tag = arrived[2 * band, 2 * rows :, :].astype(F32)
            block = jnp.max(tag).astype(jnp.int32)
            block_ref[band] = block

        @pl.loop(0, bands // PIECES, unroll=2)
        def _(j):
            band = piece * (bands // PIECES) + j
            block = block_ref[band]
            for part in range(2):
                for column in range(2):
                    at = (2 * part + column) * lanes
                    acc[block, :, at : at + lanes] += arrived[
                        2 * band + part, column * rows : (column + 1) * rows, :
                    ].astype(F32)

    pooled = acc[...].reshape(-1, 2 * width).astype(BF16)
    mine, theirs = mine_ref[...], theirs_ref[...]
    hidden = []
    for sw, pw in ((self_w, pool_w), (self_o, pool_o)):
        inner = (
            dot(mine, sw[half(core, width), :]) + dot(theirs, sw[half(1 - core, width), :]) + dot(pooled, pw[...])
        )
        hidden.append(silu(inner).astype(BF16))
    full = 2 * width
    sent = dot(hidden[0], out_w[:, full:]) + dot(hidden[1], out_o[:, full:])
    source[...] = sent.astype(BF16).reshape(source.shape)

    size = 2 * bands // PIECES

    def leave(k):
        at = pl.ds(k * size, size)
        return pltpu.make_async_copy(outgoing.at[at], outgoing_hbm.at[at], out_sem.at[k])

    @pl.loop(0, PIECES)
    def _(piece):
        @pl.loop(0, bands // PIECES, unroll=4)
        def _(j):
            band = piece * (bands // PIECES) + j
            block = block_ref[band]
            for part in range(2):
                outgoing[2 * band + part] = source[block, :, part * width : (part + 1) * width]

        leave(piece).start()

    state[...] = dot(hidden[0], out_w[:, :full]) + dot(hidden[1], out_o[:, :full])
    keep[...] = (mine.astype(F32) + state[:, half(core, width)]).astype(BF16)
    send[...] = (theirs.astype(F32) + state[:, half(1 - core, width)]).astype(BF16)
    for piece in range(PIECES):
        leave(piece).wait()


def mesh_update(arrived, core, mesh, mesh_other, weights, blocks):
    pieces, height, lanes = arrived.shape
    rows, width = (height - TAG) // 2, 2 * lanes
    flat = jax.ShapeDtypeStruct(mesh.shape, BF16)
    leaving = (pieces, rows, width)
    dma = pltpu.SemaphoreType.DMA
    return pl.pallas_call(
        mesh_body,
        out_shape=(flat, flat, pltpu.HBM(leaving, BF16)),
        grid_spec=pltpu.PrefetchScalarGridSpec(
            num_scalar_prefetch=1,
            in_specs=[hbm()] + [vmem()] * 8,
            out_specs=[vmem(), vmem(), hbm()],
            scratch_shapes=[
                pltpu.VMEM(arrived.shape, BF16),
                pltpu.VMEM((blocks, rows, 2 * width), F32),
                pltpu.VMEM((blocks * rows, 2 * width), F32),
                pltpu.VMEM((blocks, rows, 2 * width), BF16),
                pltpu.VMEM(leaving, BF16),
                pltpu.SMEM((pieces // 2,), jnp.int32),
                dma((PIECES,)),
                dma((PIECES,)),
            ],
        ),
        compiler_params=NARROW,
        cost_estimate=pl.CostEstimate(flops=10**9, bytes_accessed=12 * MB, transcendentals=1 << 17),
        name="mesh_update",
    )(core, *stay(arrived), mesh, mesh_other, *weights)


def decode_body(
    slot_ref, target_ref, picked_hbm, grid_hbm, tiles_hbm, out_hbm,
    picked, start, tiles, acc, out, picked_sem, start_sem, tiles_sem, out_sem,
):
    count = tiles.shape[0]
    blocks = acc.shape[0]
    start_start, start_ready = fetch(grid_hbm, start, start_sem, PIECES)
    picked_start, picked_ready = fetch(picked_hbm, picked, picked_sem, PIECES)
    tiles_start, tiles_ready = fetch(tiles_hbm, tiles, tiles_sem, PIECES)
    per = blocks // PIECES
    for begin in (start_start, picked_start):
        for piece in range(PIECES):
            begin(piece)
    tiles_start(0)

    @pl.loop(0, PIECES)
    def _(piece):
        start_ready(piece)

        @pl.loop(0, per, unroll=4)
        def _(j):
            acc[piece * per + j] = start[piece * per + j].astype(F32)

    for piece in range(PIECES):
        picked_ready(piece)
    for piece in range(1, PIECES):
        tiles_start(piece)

    @pl.loop(0, PIECES)
    def _(piece):
        tiles_ready(piece)

        @pl.loop(0, count // PIECES // UNROLL)
        def _(j):
            base = piece * (count // PIECES) + j * UNROLL
            for i in range(UNROLL):
                acc[target_ref[base + i]] += dot(tiles[base + i], picked[slot_ref[base + i]])

    def leave(k):
        at = pl.ds(k * per, per)
        return pltpu.make_async_copy(out.at[at], out_hbm.at[at], out_sem.at[k])

    @pl.loop(0, PIECES)
    def _(piece):
        @pl.loop(0, per, unroll=4)
        def _(j):
            out[piece * per + j] = acc[piece * per + j].astype(BF16)

        leave(piece).start()

    for piece in range(PIECES):
        leave(piece).wait()


def decode(picked, grid_blocks, tiles, slot, target):
    count, edge, _ = tiles.shape
    width = grid_blocks.shape[2]
    dma = pltpu.SemaphoreType.DMA
    return pl.pallas_call(
        decode_body,
        out_shape=jax.ShapeDtypeStruct(grid_blocks.shape, BF16),
        grid_spec=pltpu.PrefetchScalarGridSpec(
            num_scalar_prefetch=2,
            in_specs=[hbm()] * 3,
            out_specs=hbm(),
            scratch_shapes=[
                pltpu.VMEM(picked.shape, BF16),
                pltpu.VMEM(grid_blocks.shape, BF16),
                pltpu.VMEM(tiles.shape, BF16),
                pltpu.VMEM(grid_blocks.shape, F32),
                pltpu.VMEM(grid_blocks.shape, BF16),
                *[dma((PIECES,))] * 4,
            ],
        ),
        compiler_params=WIDE,
        cost_estimate=pl.CostEstimate(
            flops=2 * count * edge * edge * width, bytes_accessed=16 * MB, transcendentals=0
        ),
        name="decode",
    )(slot, target, *stay(picked, grid_blocks, tiles))


def swap(x):
    return lax.ppermute(x, "mp", SWAP)


def per_device(
    grid_nodes,
    mesh_nodes,
    send_weight,
    self_weight,
    pooled_weight,
    out_weight,
    encode_source,
    encode_slot,
    encode_tiles,
    slot_block,
    decode_slot,
    decode_target,
    decode_tiles,
):
    bands = lax.axis_size("band")
    core = lax.axis_index("mp").astype(jnp.int32)
    core_1 = core.reshape(1)
    edge = encode_tiles.shape[1]
    width = grid_nodes.shape[1]
    mesh_blocks = mesh_nodes.shape[0] // edge
    rows = edge // 2

    grid_other = swap(grid_nodes)
    halves = mesh_nodes.reshape(mesh_blocks, 2, rows, width)
    mesh_keep = lax.dynamic_index_in_dim(halves, core, 1, keepdims=False).reshape(-1, width)
    mesh_send = lax.dynamic_index_in_dim(halves, 1 - core, 1, keepdims=False).reshape(-1, width)
    out_flat = out_weight.reshape(out_weight.shape[0], -1)
    mesh_other = swap(mesh_send)
    self_other, pooled_other, out_other = swap(self_weight), swap(pooled_weight), swap(out_flat)

    slot_sums = encode(
        grid_nodes, grid_other, send_weight, encode_tiles, encode_source, encode_slot, slot_block[0], core_1, bands
    )
    arrived = lax.all_to_all(slot_sums, ("band", "mp"), split_axis=0, concat_axis=0, tiled=True)
    keep, send, outgoing = mesh_update(
        arrived,
        core_1,
        mesh_keep,
        mesh_other,
        (self_weight, self_other, pooled_weight, pooled_other, out_flat, out_other),
        mesh_blocks,
    )
    returned = lax.all_to_all(outgoing, ("band", "mp"), split_axis=0, concat_axis=0, tiled=True)
    came = swap(send).reshape(mesh_blocks, 1, rows, width)
    kept = keep.reshape(mesh_blocks, 1, rows, width)
    mesh_state = jnp.concatenate(
        [jnp.where(core == 0, kept, came), jnp.where(core == 0, came, kept)], axis=1
    ).reshape(mesh_nodes.shape)
    grid_state = decode(
        returned.reshape(bands, edge, width),
        grid_nodes.reshape(-1, edge, width),
        decode_tiles,
        decode_slot,
        decode_target,
    )
    return grid_state.reshape(grid_nodes.shape), mesh_state


def solution(mesh):
    return jax.shard_map(
        per_device,
        mesh=mesh,
        in_specs=(
            P("band", "mp"),
            P("band", "mp"),
            P(None, "mp"),
            P(None, "mp"),
            P(None, "mp"),
            P("mp", None, None),
            P("band"),
            P("band"),
            P("band", None, None),
            P("band", None),
            P("band"),
            P("band"),
            P("band", None, None),
        ),
        out_specs=(P("band", "mp"), P("band", "mp")),
        check_vma=False,
    )
```

```python
import functools

import jax
import jax.numpy as jnp
from jax import lax
from jax.experimental import pallas as pl
from jax.experimental.pallas import tpu as pltpu
from jax.sharding import PartitionSpec as P

MB = 1 << 20
F32 = jnp.float32
BF16 = jnp.bfloat16
SWAP = [(0, 1), (1, 0)]


def silu(v):
    return v / (1.0 + jnp.exp(-v))


def dot(a, b):
    return jnp.dot(a, b, preferred_element_type=F32)


def half(i, width):
    return pl.ds(pl.multiple_of(i * width, width), width)


def fetch(source, target, semaphores, count):
    size = source.shape[0] // count

    def piece(k):
        rows = pl.ds(k * size, size)
        return pltpu.make_async_copy(source.at[rows], target.at[rows], semaphores.at[k])

    return lambda k: piece(k).start(), lambda k: piece(k).wait()


def hbm():
    return pl.BlockSpec(memory_space=pltpu.HBM)


def stay(*arrays):
    return tuple(pltpu.with_memory_space_constraint(a, pltpu.HBM) for a in arrays)


def vmem():
    return pl.BlockSpec(memory_space=pltpu.VMEM)


NARROW = pltpu.CompilerParams(vmem_limit_bytes=44 * MB)


def load_body(count, *refs):
    sources, targets, semaphores = refs[:count], refs[-count - 1 : -1], refs[-1]
    copies = [pltpu.make_async_copy(x, y, semaphores.at[k]) for k, (x, y) in enumerate(zip(sources, targets))]
    for copy in copies:
        copy.start()
    for copy in copies:
        copy.wait()


def load(name, arrays, after=()):
    count = len(arrays)
    return pl.pallas_call(
        functools.partial(load_body, count),
        out_shape=tuple(pltpu.VMEM(a.shape, a.dtype) for a in arrays),
        in_specs=[hbm()] * (count + len(after)),
        out_specs=tuple(vmem() for _ in arrays),
        scratch_shapes=[pltpu.SemaphoreType.DMA((count,))],
        compiler_params=pltpu.CompilerParams(vmem_limit_bytes=24 * MB),
        cost_estimate=pl.CostEstimate(flops=0, bytes_accessed=16 * MB, transcendentals=0),
        name=name,
    )(*stay(*arrays), *stay(*after))


PIECES = 4
UNROLL = 48
TAG = 8


def encode_body(
    slot_ref, source_ref, link_ref, core_ref, own, other, weight, tiles, out_hbm, message, acc, out, out_sem,
):
    core = core_ref[0]
    blocks, edge, width = message.shape
    slots = acc.shape[0]
    count = tiles.shape[0]
    rows = edge // 2
    lanes = out.shape[2]
    inner = 8 * edge
    per = blocks * edge // inner // PIECES
    cleared = slots // (per * PIECES)

    @pl.loop(0, PIECES)
    def _(piece):
        @pl.loop(0, per)
        def _(j):
            step = piece * per + j
            at = pl.ds(pl.multiple_of(step * inner, inner), inner)
            z = dot(own[at, :], weight[half(core, width), :]) + dot(other[at, :], weight[half(1 - core, width), :])
            message[pl.ds(step * 8, 8)] = silu(z).astype(BF16).reshape(8, edge, width)
            acc[pl.ds(step * cleared, cleared)] = jnp.zeros((cleared, edge, width), F32)

    @pl.loop(0, PIECES)
    def _(piece):
        @pl.loop(0, count // PIECES // UNROLL)
        def _(j):
            base = piece * (count // PIECES) + j * UNROLL
            for i in range(UNROLL):
                acc[slot_ref[base + i]] += dot(tiles[base + i], message[source_ref[base + i]])

    size = 2 * slots // PIECES

    def leave(k):
        at = pl.ds(k * size, size)
        return pltpu.make_async_copy(out.at[at], out_hbm.at[at], out_sem.at[k])

    @pl.loop(0, PIECES)
    def _(piece):
        @pl.loop(0, slots // PIECES, unroll=4)
        def _(j):
            slot = piece * (slots // PIECES) + j
            tag = jnp.full((TAG, lanes), link_ref[slot].astype(F32), F32).astype(BF16)
            for part in range(2):
                value = acc[slot, part * rows : (part + 1) * rows, :].astype(BF16)
                for column in range(2):
                    out[2 * slot + part, column * rows : (column + 1) * rows, :] = value[
                        :, column * lanes : (column + 1) * lanes
                    ]
                out[2 * slot + part, 2 * rows :, :] = tag

        leave(piece).start()

    for piece in range(PIECES):
        leave(piece).wait()


def encode(own, other, weight, tiles, source, slot, link, core, slots):
    count, edge, _ = tiles.shape
    width = weight.shape[1]
    sent = (2 * slots, edge + TAG, width // 2)
    dma = pltpu.SemaphoreType.DMA
    return pl.pallas_call(
        encode_body,
        out_shape=pltpu.HBM(sent, BF16),
        grid_spec=pltpu.PrefetchScalarGridSpec(
            num_scalar_prefetch=4,
            in_specs=[vmem()] * 4,
            out_specs=hbm(),
            scratch_shapes=[
                pltpu.VMEM((own.shape[0] // edge, edge, width), BF16),
                pltpu.VMEM((slots, edge, width), F32),
                pltpu.VMEM(sent, BF16),
                dma((PIECES,)),
            ],
        ),
        compiler_params=pltpu.CompilerParams(vmem_limit_bytes=32 * MB),
        cost_estimate=pl.CostEstimate(
            flops=2 * count * edge * edge * width, bytes_accessed=16 * MB, transcendentals=own.shape[0] * width
        ),
        name="encode",
    )(slot, source, link, core, own, other, weight, tiles)


def mesh_body(
    core_ref, arrived_hbm, mine_ref, theirs_ref, self_w, self_o, pool_w, pool_o, out_w, out_o, keep, send,
    outgoing_hbm, arrived, acc, state, source, outgoing, block_ref, arrived_sem, out_sem,
):
    core = core_ref[0]
    bands = arrived.shape[0] // 2
    lanes = arrived.shape[2]
    rows = acc.shape[1]
    width = 2 * lanes
    arrived_start, ready = fetch(arrived_hbm, arrived, arrived_sem, PIECES)
    for piece in range(PIECES):
        arrived_start(piece)
    acc[...] = jnp.zeros(acc.shape, F32)

    @pl.loop(0, PIECES)
    def _(piece):
        ready(piece)

        @pl.loop(0, bands // PIECES, unroll=16)
        def _(j):
            band = piece * (bands // PIECES) + j
            tag = arrived[2 * band, 2 * rows :, :].astype(F32)
            block = jnp.max(tag).astype(jnp.int32)
            block_ref[band] = block

        @pl.loop(0, bands // PIECES, unroll=2)
        def _(j):
            band = piece * (bands // PIECES) + j
            block = block_ref[band]
            for part in range(2):
                for column in range(2):
                    at = (2 * part + column) * lanes
                    acc[block, :, at : at + lanes] += arrived[
                        2 * band + part, column * rows : (column + 1) * rows, :
                    ].astype(F32)

    pooled = acc[...].reshape(-1, 2 * width).astype(BF16)
    mine, theirs = mine_ref[...], theirs_ref[...]
    hidden = []
    for sw, pw in ((self_w, pool_w), (self_o, pool_o)):
        inner = (
            dot(mine, sw[half(core, width), :]) + dot(theirs, sw[half(1 - core, width), :]) + dot(pooled, pw[...])
        )
        hidden.append(silu(inner).astype(BF16))
    full = 2 * width
    sent = dot(hidden[0], out_w[:, full:]) + dot(hidden[1], out_o[:, full:])
    source[...] = sent.astype(BF16).reshape(source.shape)

    size = 2 * bands // PIECES

    def leave(k):
        at = pl.ds(k * size, size)
        return pltpu.make_async_copy(outgoing.at[at], outgoing_hbm.at[at], out_sem.at[k])

    @pl.loop(0, PIECES)
    def _(piece):
        @pl.loop(0, bands // PIECES, unroll=4)
        def _(j):
            band = piece * (bands // PIECES) + j
            block = block_ref[band]
            for part in range(2):
                outgoing[2 * band + part] = source[block, :, part * width : (part + 1) * width]

        leave(piece).start()

    state[...] = dot(hidden[0], out_w[:, :full]) + dot(hidden[1], out_o[:, :full])
    keep[...] = (mine.astype(F32) + state[:, half(core, width)]).astype(BF16)
    send[...] = (theirs.astype(F32) + state[:, half(1 - core, width)]).astype(BF16)
    for piece in range(PIECES):
        leave(piece).wait()


def mesh_update(arrived, core, mesh, mesh_other, weights, blocks):
    pieces, height, lanes = arrived.shape
    rows, width = (height - TAG) // 2, 2 * lanes
    flat = jax.ShapeDtypeStruct(mesh.shape, BF16)
    leaving = (pieces, rows, width)
    dma = pltpu.SemaphoreType.DMA
    return pl.pallas_call(
        mesh_body,
        out_shape=(flat, flat, pltpu.HBM(leaving, BF16)),
        grid_spec=pltpu.PrefetchScalarGridSpec(
            num_scalar_prefetch=1,
            in_specs=[hbm()] + [vmem()] * 8,
            out_specs=[vmem(), vmem(), hbm()],
            scratch_shapes=[
                pltpu.VMEM(arrived.shape, BF16),
                pltpu.VMEM((blocks, rows, 2 * width), F32),
                pltpu.VMEM((blocks * rows, 2 * width), F32),
                pltpu.VMEM((blocks, rows, 2 * width), BF16),
                pltpu.VMEM(leaving, BF16),
                pltpu.SMEM((pieces // 2,), jnp.int32),
                dma((PIECES,)),
                dma((PIECES,)),
            ],
        ),
        compiler_params=NARROW,
        cost_estimate=pl.CostEstimate(flops=10**9, bytes_accessed=12 * MB, transcendentals=1 << 17),
        name="mesh_update",
    )(core, *stay(arrived), mesh, mesh_other, *weights)


def decode_body(
    slot_ref, target_ref, picked_hbm, start, tiles_hbm, out_hbm,
    picked, tiles, acc, out, picked_sem, tiles_sem, out_sem,
):
    count = tiles.shape[0]
    blocks = acc.shape[0]
    picked_start, picked_ready = fetch(picked_hbm, picked, picked_sem, PIECES)
    tiles_start, tiles_ready = fetch(tiles_hbm, tiles, tiles_sem, PIECES)
    per = blocks // PIECES
    for piece in range(PIECES):
        picked_start(piece)
    for piece in range(PIECES):
        tiles_start(piece)

    @pl.loop(0, PIECES)
    def _(piece):
        @pl.loop(0, per, unroll=4)
        def _(j):
            acc[piece * per + j] = start[piece * per + j].astype(F32)

    for piece in range(PIECES):
        picked_ready(piece)

    @pl.loop(0, PIECES)
    def _(piece):
        tiles_ready(piece)

        @pl.loop(0, count // PIECES // UNROLL)
        def _(j):
            base = piece * (count // PIECES) + j * UNROLL
            for i in range(UNROLL):
                acc[target_ref[base + i]] += dot(tiles[base + i], picked[slot_ref[base + i]])

    def leave(k):
        at = pl.ds(k * per, per)
        return pltpu.make_async_copy(out.at[at], out_hbm.at[at], out_sem.at[k])

    @pl.loop(0, PIECES)
    def _(piece):
        @pl.loop(0, per, unroll=4)
        def _(j):
            out[piece * per + j] = acc[piece * per + j].astype(BF16)

        leave(piece).start()

    for piece in range(PIECES):
        leave(piece).wait()


def decode(picked, grid_blocks, tiles, slot, target):
    count, edge, _ = tiles.shape
    width = grid_blocks.shape[2]
    dma = pltpu.SemaphoreType.DMA
    return pl.pallas_call(
        decode_body,
        out_shape=jax.ShapeDtypeStruct(grid_blocks.shape, BF16),
        grid_spec=pltpu.PrefetchScalarGridSpec(
            num_scalar_prefetch=2,
            in_specs=[hbm(), vmem(), hbm()],
            out_specs=hbm(),
            scratch_shapes=[
                pltpu.VMEM(picked.shape, BF16),
                pltpu.VMEM(tiles.shape, BF16),
                pltpu.VMEM(grid_blocks.shape, F32),
                pltpu.VMEM(grid_blocks.shape, BF16),
                *[dma((PIECES,))] * 3,
            ],
        ),
        compiler_params=pltpu.CompilerParams(vmem_limit_bytes=40 * MB),
        cost_estimate=pl.CostEstimate(
            flops=2 * count * edge * edge * width, bytes_accessed=16 * MB, transcendentals=0
        ),
        name="decode",
    )(slot, target, *stay(picked), grid_blocks, *stay(tiles))


def swap(x):
    return lax.ppermute(x, "mp", SWAP)


def per_device(
    grid_nodes,
    mesh_nodes,
    send_weight,
    self_weight,
    pooled_weight,
    out_weight,
    encode_source,
    encode_slot,
    encode_tiles,
    slot_block,
    decode_slot,
    decode_target,
    decode_tiles,
):
    bands = lax.axis_size("band")
    core = lax.axis_index("mp").astype(jnp.int32)
    core_1 = core.reshape(1)
    edge = encode_tiles.shape[1]
    width = grid_nodes.shape[1]
    mesh_blocks = mesh_nodes.shape[0] // edge
    rows = edge // 2

    grid_other = swap(grid_nodes)
    halves = mesh_nodes.reshape(mesh_blocks, 2, rows, width)
    mesh_keep = lax.dynamic_index_in_dim(halves, core, 1, keepdims=False).reshape(-1, width)
    mesh_send = lax.dynamic_index_in_dim(halves, 1 - core, 1, keepdims=False).reshape(-1, width)
    out_flat = out_weight.reshape(out_weight.shape[0], -1)
    mesh_other = swap(mesh_send)
    self_other, pooled_other, out_other = swap(self_weight), swap(pooled_weight), swap(out_flat)

    own, near_weight, near_tiles = load("load_encode", (grid_nodes, send_weight, encode_tiles))
    slot_sums = encode(
        own, grid_other, near_weight, near_tiles, encode_source, encode_slot, slot_block[0], core_1, bands
    )
    arrived = lax.all_to_all(slot_sums, ("band", "mp"), split_axis=0, concat_axis=0, tiled=True)
    keep, send, outgoing = mesh_update(
        arrived,
        core_1,
        mesh_keep,
        mesh_other,
        (self_weight, self_other, pooled_weight, pooled_other, out_flat, out_other),
        mesh_blocks,
    )
    returned = lax.all_to_all(outgoing, ("band", "mp"), split_axis=0, concat_axis=0, tiled=True)
    came = swap(send)
    came = came.reshape(mesh_blocks, 1, rows, width)
    kept = keep.reshape(mesh_blocks, 1, rows, width)
    mesh_state = jnp.concatenate(
        [jnp.where(core == 0, kept, came), jnp.where(core == 0, came, kept)], axis=1
    ).reshape(mesh_nodes.shape)
    grid_state = decode(
        returned.reshape(bands, edge, width),
        grid_nodes.reshape(-1, edge, width),
        decode_tiles,
        decode_slot,
        decode_target,
    )
    return grid_state.reshape(grid_nodes.shape), mesh_state


def solution(mesh):
    return jax.shard_map(
        per_device,
        mesh=mesh,
        in_specs=(
            P("band", "mp"),
            P("band", "mp"),
            P(None, "mp"),
            P(None, "mp"),
            P(None, "mp"),
            P("mp", None, None),
            P("band"),
            P("band"),
            P("band", None, None),
            P("band", None),
            P("band"),
            P("band"),
            P("band", None, None),
        ),
        out_specs=(P("band", "mp"), P("band", "mp")),
        check_vma=False,
    )
```

```python
import functools

import jax
import jax.numpy as jnp
from jax import lax
from jax.experimental import pallas as pl
from jax.experimental.pallas import tpu as pltpu
from jax.sharding import PartitionSpec as P

MB = 1 << 20
F32 = jnp.float32
BF16 = jnp.bfloat16
SWAP = [(0, 1), (1, 0)]


def silu(v):
    return v / (1.0 + jnp.exp(-v))


def dot(a, b):
    return jnp.dot(a, b, preferred_element_type=F32)


def half(i, width):
    return pl.ds(pl.multiple_of(i * width, width), width)


def fetch(source, target, semaphores, count):
    size = source.shape[0] // count

    def piece(k):
        rows = pl.ds(k * size, size)
        return pltpu.make_async_copy(source.at[rows], target.at[rows], semaphores.at[k])

    return lambda k: piece(k).start(), lambda k: piece(k).wait()


def hbm():
    return pl.BlockSpec(memory_space=pltpu.HBM)


def stay(*arrays):
    return tuple(pltpu.with_memory_space_constraint(a, pltpu.HBM) for a in arrays)


def vmem():
    return pl.BlockSpec(memory_space=pltpu.VMEM)


NARROW = pltpu.CompilerParams(vmem_limit_bytes=44 * MB)


def pair_up(key_ref, begin, count, table, row, pending, missing):
    keys = pending.shape[0]

    @pl.loop(0, keys, unroll=16)
    def _(k):
        pending[k] = -1

    def visit(t, n):
        key = key_ref[begin + t]
        waiting = pending[key]
        both = waiting >= 0
        table[row, n] = waiting
        table[row + 1, n] = begin + t
        pending[key] = jnp.where(both, -1, begin + t)
        return n + both.astype(jnp.int32)

    def leave(k, n):
        waiting = pending[k]
        table[row, n] = waiting
        table[row + 1, n] = missing
        return n + (waiting >= 0).astype(jnp.int32)

    n = lax.fori_loop(0, count, visit, jnp.int32(0), unroll=8)
    n = lax.fori_loop(0, keys, leave, n, unroll=8)

    @pl.loop(0, GROUP, unroll=8)
    def _(k):
        table[row, n + k] = missing
        table[row + 1, n + k] = missing

    table[row + 2, 0] = (n + GROUP - 1) // GROUP


def products(table, row, first, tiles, sums, sum_ref, rows, row_ref):
    last = row_ref.shape[0] - 1
    for i in range(GROUP):
        one, two = table[row, first + i], table[row + 1, first + i]
        near, far = jnp.minimum(one, last), jnp.minimum(two, last)
        both = jnp.concatenate([tiles[one], tiles[two]], axis=1)
        under = jnp.concatenate([rows[row_ref[near]], rows[row_ref[far]]], axis=0)
        sums[sum_ref[near]] += dot(both, under)


def load_body(key_ref, own_hbm, weight_hbm, tiles_hbm, own, weight, tiles, table, pending, semaphores):
    count = tiles_hbm.shape[0]
    moves = ((own_hbm, own), (weight_hbm, weight), (tiles_hbm, tiles.at[pl.ds(0, count)]))
    copies = [pltpu.make_async_copy(x, y, semaphores.at[k]) for k, (x, y) in enumerate(moves)]
    for copy in copies:
        copy.start()
    tiles[count:] = jnp.zeros((tiles.shape[0] - count, *tiles.shape[1:]), BF16)
    pair_up(key_ref, 0, count, table, 0, pending, count)
    for copy in copies:
        copy.wait()


def pair_body(parts, key_ref, after, table, pending):
    count = key_ref.shape[0]
    for k in range(parts):
        pair_up(key_ref, k * (count // parts), count // parts, table, 3 * k, pending, count)


def pairs(key, keys, parts, after):
    return pl.pallas_call(
        functools.partial(pair_body, parts),
        out_shape=jax.ShapeDtypeStruct((8, TABLE), jnp.int32),
        in_specs=[pl.BlockSpec(memory_space=pltpu.SMEM), hbm()],
        out_specs=pl.BlockSpec(memory_space=pltpu.SMEM),
        scratch_shapes=[pltpu.SMEM((keys,), jnp.int32)],
        cost_estimate=pl.CostEstimate(flops=0, bytes_accessed=8 * MB, transcendentals=0),
        name="pair_decode",
    )(key, *stay(after))


def load(key, keys, own, weight, tiles):
    padded = (tiles.shape[0] + 8, *tiles.shape[1:])
    return pl.pallas_call(
        load_body,
        out_shape=(
            pltpu.VMEM(own.shape, BF16),
            pltpu.VMEM(weight.shape, BF16),
            pltpu.VMEM(padded, BF16),
            jax.ShapeDtypeStruct((8, TABLE), jnp.int32),
        ),
        in_specs=[pl.BlockSpec(memory_space=pltpu.SMEM), hbm(), hbm(), hbm()],
        out_specs=(vmem(), vmem(), vmem(), pl.BlockSpec(memory_space=pltpu.SMEM)),
        scratch_shapes=[pltpu.SMEM((keys,), jnp.int32), pltpu.SemaphoreType.DMA((3,))],
        compiler_params=pltpu.CompilerParams(vmem_limit_bytes=24 * MB),
        cost_estimate=pl.CostEstimate(flops=0, bytes_accessed=16 * MB, transcendentals=0),
        name="load_encode",
    )(key, *stay(own, weight, tiles))


PIECES = 4
GROUP = 32
TABLE = 256
PARTS = 2
TAG = 8


def encode_body(
    table, slot_ref, source_ref, link_ref, core_ref, own, other, weight, tiles, out_hbm, message, acc, out, out_sem,
):
    core = core_ref[0]
    blocks, edge, width = message.shape
    slots = acc.shape[0]
    rows = edge // 2
    lanes = out.shape[2]
    inner = 8 * edge
    per = blocks * edge // inner // PIECES
    cleared = slots // (per * PIECES)

    @pl.loop(0, PIECES)
    def _(piece):
        @pl.loop(0, per)
        def _(j):
            step = piece * per + j
            at = pl.ds(pl.multiple_of(step * inner, inner), inner)
            z = dot(own[at, :], weight[half(core, width), :]) + dot(other[at, :], weight[half(1 - core, width), :])
            message[pl.ds(step * 8, 8)] = silu(z).astype(BF16).reshape(8, edge, width)
            acc[pl.ds(step * cleared, cleared)] = jnp.zeros((cleared, edge, width), F32)

    @pl.loop(0, table[2, 0])
    def _(j):
        products(table, 0, j * GROUP, tiles, acc, slot_ref, message, source_ref)

    size = 2 * slots // PIECES

    def leave(k):
        at = pl.ds(k * size, size)
        return pltpu.make_async_copy(out.at[at], out_hbm.at[at], out_sem.at[k])

    @pl.loop(0, PIECES)
    def _(piece):
        @pl.loop(0, slots // PIECES, unroll=4)
        def _(j):
            slot = piece * (slots // PIECES) + j
            tag = jnp.full((TAG, lanes), link_ref[slot].astype(F32), F32).astype(BF16)
            for part in range(2):
                value = acc[slot, part * rows : (part + 1) * rows, :].astype(BF16)
                for column in range(2):
                    out[2 * slot + part, column * rows : (column + 1) * rows, :] = value[
                        :, column * lanes : (column + 1) * lanes
                    ]
                out[2 * slot + part, 2 * rows :, :] = tag

        leave(piece).start()

    for piece in range(PIECES):
        leave(piece).wait()


def encode(own, other, weight, tiles, table, source, slot, link, core, slots):
    count, edge, _ = tiles.shape
    width = weight.shape[1]
    sent = (2 * slots, edge + TAG, width // 2)
    dma = pltpu.SemaphoreType.DMA
    return pl.pallas_call(
        encode_body,
        out_shape=pltpu.HBM(sent, BF16),
        grid_spec=pltpu.PrefetchScalarGridSpec(
            num_scalar_prefetch=5,
            in_specs=[vmem()] * 4,
            out_specs=hbm(),
            scratch_shapes=[
                pltpu.VMEM((own.shape[0] // edge, edge, width), BF16),
                pltpu.VMEM((slots, edge, width), F32),
                pltpu.VMEM(sent, BF16),
                dma((PIECES,)),
            ],
        ),
        compiler_params=pltpu.CompilerParams(vmem_limit_bytes=32 * MB),
        cost_estimate=pl.CostEstimate(
            flops=2 * count * edge * edge * width, bytes_accessed=16 * MB, transcendentals=own.shape[0] * width
        ),
        name="encode",
    )(table, slot, source, link, core, own, other, weight, tiles)


def mesh_body(
    core_ref, arrived_hbm, mine_ref, theirs_ref, self_w, self_o, pool_w, pool_o, out_w, out_o, keep, send,
    outgoing_hbm, arrived, acc, state, source, outgoing, block_ref, arrived_sem, out_sem,
):
    core = core_ref[0]
    bands = arrived.shape[0] // 2
    lanes = arrived.shape[2]
    rows = acc.shape[1]
    width = 2 * lanes
    arrived_start, ready = fetch(arrived_hbm, arrived, arrived_sem, PIECES)
    for piece in range(PIECES):
        arrived_start(piece)
    acc[...] = jnp.zeros(acc.shape, F32)

    @pl.loop(0, PIECES)
    def _(piece):
        ready(piece)

        @pl.loop(0, bands // PIECES, unroll=16)
        def _(j):
            band = piece * (bands // PIECES) + j
            tag = arrived[2 * band, 2 * rows :, :].astype(F32)
            block = jnp.max(tag).astype(jnp.int32)
            block_ref[band] = block

        @pl.loop(0, bands // PIECES, unroll=2)
        def _(j):
            band = piece * (bands // PIECES) + j
            block = block_ref[band]
            for part in range(2):
                for column in range(2):
                    at = (2 * part + column) * lanes
                    acc[block, :, at : at + lanes] += arrived[
                        2 * band + part, column * rows : (column + 1) * rows, :
                    ].astype(F32)

    pooled = acc[...].reshape(-1, 2 * width).astype(BF16)
    mine, theirs = mine_ref[...], theirs_ref[...]
    hidden = []
    for sw, pw in ((self_w, pool_w), (self_o, pool_o)):
        inner = (
            dot(mine, sw[half(core, width), :]) + dot(theirs, sw[half(1 - core, width), :]) + dot(pooled, pw[...])
        )
        hidden.append(silu(inner).astype(BF16))
    full = 2 * width
    sent = dot(hidden[0], out_w[:, full:]) + dot(hidden[1], out_o[:, full:])
    source[...] = sent.astype(BF16).reshape(source.shape)

    size = 2 * bands // PIECES

    def leave(k):
        at = pl.ds(k * size, size)
        return pltpu.make_async_copy(outgoing.at[at], outgoing_hbm.at[at], out_sem.at[k])

    @pl.loop(0, PIECES)
    def _(piece):
        @pl.loop(0, bands // PIECES, unroll=4)
        def _(j):
            band = piece * (bands // PIECES) + j
            block = block_ref[band]
            for part in range(2):
                outgoing[2 * band + part] = source[block, :, part * width : (part + 1) * width]

        leave(piece).start()

    state[...] = dot(hidden[0], out_w[:, :full]) + dot(hidden[1], out_o[:, :full])
    keep[...] = (mine.astype(F32) + state[:, half(core, width)]).astype(BF16)
    send[...] = (theirs.astype(F32) + state[:, half(1 - core, width)]).astype(BF16)
    for piece in range(PIECES):
        leave(piece).wait()


def mesh_update(arrived, core, mesh, mesh_other, weights, blocks):
    pieces, height, lanes = arrived.shape
    rows, width = (height - TAG) // 2, 2 * lanes
    flat = jax.ShapeDtypeStruct(mesh.shape, BF16)
    leaving = (pieces, rows, width)
    dma = pltpu.SemaphoreType.DMA
    return pl.pallas_call(
        mesh_body,
        out_shape=(flat, flat, pltpu.HBM(leaving, BF16)),
        grid_spec=pltpu.PrefetchScalarGridSpec(
            num_scalar_prefetch=1,
            in_specs=[hbm()] + [vmem()] * 8,
            out_specs=[vmem(), vmem(), hbm()],
            scratch_shapes=[
                pltpu.VMEM(arrived.shape, BF16),
                pltpu.VMEM((blocks, rows, 2 * width), F32),
                pltpu.VMEM((blocks * rows, 2 * width), F32),
                pltpu.VMEM((blocks, rows, 2 * width), BF16),
                pltpu.VMEM(leaving, BF16),
                pltpu.SMEM((pieces // 2,), jnp.int32),
                dma((PIECES,)),
                dma((PIECES,)),
            ],
        ),
        compiler_params=NARROW,
        cost_estimate=pl.CostEstimate(flops=10**9, bytes_accessed=12 * MB, transcendentals=1 << 17),
        name="mesh_update",
    )(core, *stay(arrived), mesh, mesh_other, *weights)


def decode_body(
    table, slot_ref, target_ref, picked_hbm, start, tiles_hbm, out_hbm,
    picked, tiles, acc, out, picked_sem, tiles_sem, out_sem,
):
    count = tiles_hbm.shape[0]
    blocks = acc.shape[0]
    picked_start, picked_ready = fetch(picked_hbm, picked, picked_sem, PIECES)
    tiles_start, tiles_ready = fetch(tiles_hbm, tiles, tiles_sem, PARTS)
    per = blocks // PIECES
    for piece in range(PIECES):
        picked_start(piece)
    tiles_start(0)
    tiles[count:] = jnp.zeros((tiles.shape[0] - count, *tiles.shape[1:]), BF16)

    @pl.loop(0, PIECES)
    def _(piece):
        @pl.loop(0, per, unroll=4)
        def _(j):
            acc[piece * per + j] = start[piece * per + j].astype(F32)

    for piece in range(PIECES):
        picked_ready(piece)
    for part in range(1, PARTS):
        tiles_start(part)

    @pl.loop(0, PARTS)
    def _(part):
        tiles_ready(part)

        @pl.loop(0, table[3 * part + 2, 0])
        def _(j):
            products(table, 3 * part, j * GROUP, tiles, acc, target_ref, picked, slot_ref)

    def leave(k):
        at = pl.ds(k * per, per)
        return pltpu.make_async_copy(out.at[at], out_hbm.at[at], out_sem.at[k])

    @pl.loop(0, PIECES)
    def _(piece):
        @pl.loop(0, per, unroll=4)
        def _(j):
            out[piece * per + j] = acc[piece * per + j].astype(BF16)

        leave(piece).start()

    for piece in range(PIECES):
        leave(piece).wait()


def decode(picked, grid_blocks, tiles, table, slot, target):
    count, edge, _ = tiles.shape
    width = grid_blocks.shape[2]
    dma = pltpu.SemaphoreType.DMA
    return pl.pallas_call(
        decode_body,
        out_shape=jax.ShapeDtypeStruct(grid_blocks.shape, BF16),
        grid_spec=pltpu.PrefetchScalarGridSpec(
            num_scalar_prefetch=3,
            in_specs=[hbm(), vmem(), hbm()],
            out_specs=hbm(),
            scratch_shapes=[
                pltpu.VMEM(picked.shape, BF16),
                pltpu.VMEM((count + 8, edge, edge), BF16),
                pltpu.VMEM(grid_blocks.shape, F32),
                pltpu.VMEM(grid_blocks.shape, BF16),
                *[dma((PIECES,))] * 3,
            ],
        ),
        compiler_params=pltpu.CompilerParams(vmem_limit_bytes=40 * MB),
        cost_estimate=pl.CostEstimate(
            flops=2 * count * edge * edge * width, bytes_accessed=16 * MB, transcendentals=0
        ),
        name="decode",
    )(table, slot, target, *stay(picked), grid_blocks, *stay(tiles))


def swap(x):
    return lax.ppermute(x, "mp", SWAP)


def per_device(
    grid_nodes,
    mesh_nodes,
    send_weight,
    self_weight,
    pooled_weight,
    out_weight,
    encode_source,
    encode_slot,
    encode_tiles,
    slot_block,
    decode_slot,
    decode_target,
    decode_tiles,
):
    bands = lax.axis_size("band")
    core = lax.axis_index("mp").astype(jnp.int32)
    core_1 = core.reshape(1)
    edge = encode_tiles.shape[1]
    width = grid_nodes.shape[1]
    mesh_blocks = mesh_nodes.shape[0] // edge
    rows = edge // 2

    grid_other = swap(grid_nodes)
    halves = mesh_nodes.reshape(mesh_blocks, 2, rows, width)
    mesh_keep = lax.dynamic_index_in_dim(halves, core, 1, keepdims=False).reshape(-1, width)
    mesh_send = lax.dynamic_index_in_dim(halves, 1 - core, 1, keepdims=False).reshape(-1, width)
    out_flat = out_weight.reshape(out_weight.shape[0], -1)
    mesh_other = swap(mesh_send)
    self_other, pooled_other, out_other = swap(self_weight), swap(pooled_weight), swap(out_flat)

    own, near_weight, near_tiles, table = load(encode_slot, bands, grid_nodes, send_weight, encode_tiles)
    slot_sums = encode(
        own, grid_other, near_weight, near_tiles, table, encode_source, encode_slot, slot_block[0], core_1, bands
    )
    arrived = lax.all_to_all(slot_sums, ("band", "mp"), split_axis=0, concat_axis=0, tiled=True)
    keep, send, outgoing = mesh_update(
        arrived,
        core_1,
        mesh_keep,
        mesh_other,
        (self_weight, self_other, pooled_weight, pooled_other, out_flat, out_other),
        mesh_blocks,
    )
    returned = lax.all_to_all(outgoing, ("band", "mp"), split_axis=0, concat_axis=0, tiled=True)
    came = swap(send)
    decode_table = pairs(decode_target, grid_nodes.shape[0] // edge, PARTS, came)
    came = came.reshape(mesh_blocks, 1, rows, width)
    kept = keep.reshape(mesh_blocks, 1, rows, width)
    mesh_state = jnp.concatenate(
        [jnp.where(core == 0, kept, came), jnp.where(core == 0, came, kept)], axis=1
    ).reshape(mesh_nodes.shape)
    grid_state = decode(
        returned.reshape(bands, edge, width),
        grid_nodes.reshape(-1, edge, width),
        decode_tiles,
        decode_table,
        decode_slot,
        decode_target,
    )
    return grid_state.reshape(grid_nodes.shape), mesh_state


def solution(mesh):
    return jax.shard_map(
        per_device,
        mesh=mesh,
        in_specs=(
            P("band", "mp"),
            P("band", "mp"),
            P(None, "mp"),
            P(None, "mp"),
            P(None, "mp"),
            P("mp", None, None),
            P("band"),
            P("band"),
            P("band", None, None),
            P("band", None),
            P("band"),
            P("band"),
            P("band", None, None),
        ),
        out_specs=(P("band", "mp"), P("band", "mp")),
        check_vma=False,
    )
```

```python
import functools

import jax
import jax.numpy as jnp
from jax import lax
from jax.experimental import pallas as pl
from jax.experimental.pallas import tpu as pltpu
from jax.sharding import PartitionSpec as P

MB = 1 << 20
F32 = jnp.float32
BF16 = jnp.bfloat16
SWAP = [(0, 1), (1, 0)]


def silu(v):
    return v / (1.0 + jnp.exp(-v))


def dot(a, b):
    return jnp.dot(a, b, preferred_element_type=F32)


def half(i, width):
    return pl.ds(pl.multiple_of(i * width, width), width)


def fetch(source, target, semaphores, count):
    size = source.shape[0] // count

    def piece(k):
        rows = pl.ds(k * size, size)
        return pltpu.make_async_copy(source.at[rows], target.at[rows], semaphores.at[k])

    return lambda k: piece(k).start(), lambda k: piece(k).wait()


def hbm():
    return pl.BlockSpec(memory_space=pltpu.HBM)


def stay(*arrays):
    return tuple(pltpu.with_memory_space_constraint(a, pltpu.HBM) for a in arrays)


def vmem():
    return pl.BlockSpec(memory_space=pltpu.VMEM)


NARROW = pltpu.CompilerParams(vmem_limit_bytes=44 * MB)


def load_body(count, *refs):
    sources, targets, semaphores = refs[:count], refs[-count - 1 : -1], refs[-1]
    copies = [pltpu.make_async_copy(x, y, semaphores.at[k]) for k, (x, y) in enumerate(zip(sources, targets))]
    for copy in copies:
        copy.start()
    for copy in copies:
        copy.wait()


def load(name, arrays, after=()):
    count = len(arrays)
    return pl.pallas_call(
        functools.partial(load_body, count),
        out_shape=tuple(pltpu.VMEM(a.shape, a.dtype) for a in arrays),
        in_specs=[hbm()] * (count + len(after)),
        out_specs=tuple(vmem() for _ in arrays),
        scratch_shapes=[pltpu.SemaphoreType.DMA((count,))],
        compiler_params=pltpu.CompilerParams(vmem_limit_bytes=24 * MB),
        cost_estimate=pl.CostEstimate(flops=0, bytes_accessed=16 * MB, transcendentals=0),
        name=name,
    )(*stay(*arrays), *stay(*after))


PIECES = 4
UNROLL = 48


def encode_body(
    slot_ref, source_ref, core_ref, own, other, weight, tiles, out_hbm, message, acc, out, out_sem,
):
    core = core_ref[0]
    blocks, edge, width = message.shape
    slots = acc.shape[0]
    count = tiles.shape[0]
    rows = edge // 2
    inner = 8 * edge
    per = blocks * edge // inner // PIECES
    cleared = slots // (per * PIECES)

    @pl.loop(0, PIECES)
    def _(piece):
        @pl.loop(0, per)
        def _(j):
            step = piece * per + j
            at = pl.ds(pl.multiple_of(step * inner, inner), inner)
            z = dot(own[at, :], weight[half(core, width), :]) + dot(other[at, :], weight[half(1 - core, width), :])
            message[pl.ds(step * 8, 8)] = silu(z).astype(BF16).reshape(8, edge, width)
            acc[pl.ds(step * cleared, cleared)] = jnp.zeros((cleared, edge, width), F32)

    @pl.loop(0, PIECES)
    def _(piece):
        @pl.loop(0, count // PIECES // UNROLL)
        def _(j):
            base = piece * (count // PIECES) + j * UNROLL
            for i in range(UNROLL):
                acc[slot_ref[base + i]] += dot(tiles[base + i], message[source_ref[base + i]])

    size = 2 * slots // PIECES

    def leave(k):
        at = pl.ds(k * size, size)
        return pltpu.make_async_copy(out.at[at], out_hbm.at[at], out_sem.at[k])

    @pl.loop(0, PIECES)
    def _(piece):
        @pl.loop(0, slots // PIECES, unroll=4)
        def _(j):
            slot = piece * (slots // PIECES) + j
            for part in range(2):
                out[2 * slot + part] = acc[slot, part * rows : (part + 1) * rows, :].astype(BF16)

        leave(piece).start()

    for piece in range(PIECES):
        leave(piece).wait()


def encode(own, other, weight, tiles, source, slot, core, slots):
    count, edge, _ = tiles.shape
    width = weight.shape[1]
    sent = (2 * slots, edge // 2, width)
    dma = pltpu.SemaphoreType.DMA
    return pl.pallas_call(
        encode_body,
        out_shape=pltpu.HBM(sent, BF16),
        grid_spec=pltpu.PrefetchScalarGridSpec(
            num_scalar_prefetch=3,
            in_specs=[vmem()] * 4,
            out_specs=hbm(),
            scratch_shapes=[
                pltpu.VMEM((own.shape[0] // edge, edge, width), BF16),
                pltpu.VMEM((slots, edge, width), F32),
                pltpu.VMEM(sent, BF16),
                dma((PIECES,)),
            ],
        ),
        compiler_params=pltpu.CompilerParams(vmem_limit_bytes=32 * MB),
        cost_estimate=pl.CostEstimate(
            flops=2 * count * edge * edge * width, bytes_accessed=16 * MB, transcendentals=own.shape[0] * width
        ),
        name="encode",
    )(slot, source, core, own, other, weight, tiles)


def mesh_body(
    block_ref, core_ref, arrived_hbm, mine_ref, theirs_ref, self_w, self_o, pool_w, pool_o, out_w, out_o, keep, send,
    outgoing_hbm, arrived, acc, state, source, outgoing, arrived_sem, out_sem,
):
    core = core_ref[0]
    bands = arrived.shape[0] // 2
    width = arrived.shape[2]
    arrived_start, ready = fetch(arrived_hbm, arrived, arrived_sem, PIECES)
    for piece in range(PIECES):
        arrived_start(piece)
    acc[...] = jnp.zeros(acc.shape, F32)

    @pl.loop(0, PIECES)
    def _(piece):
        ready(piece)

        @pl.loop(0, bands // PIECES, unroll=4)
        def _(j):
            band = piece * (bands // PIECES) + j
            block = block_ref[band]
            for part in range(2):
                acc[block, :, part * width : (part + 1) * width] += arrived[2 * band + part].astype(F32)

    pooled = acc[...].reshape(-1, 2 * width).astype(BF16)
    mine, theirs = mine_ref[...], theirs_ref[...]
    hidden = []
    for sw, pw in ((self_w, pool_w), (self_o, pool_o)):
        inner = (
            dot(mine, sw[half(core, width), :]) + dot(theirs, sw[half(1 - core, width), :]) + dot(pooled, pw[...])
        )
        hidden.append(silu(inner).astype(BF16))
    full = 2 * width
    sent = dot(hidden[0], out_w[:, full:]) + dot(hidden[1], out_o[:, full:])
    source[...] = sent.astype(BF16).reshape(source.shape)

    size = 2 * bands // PIECES

    def leave(k):
        at = pl.ds(k * size, size)
        return pltpu.make_async_copy(outgoing.at[at], outgoing_hbm.at[at], out_sem.at[k])

    @pl.loop(0, PIECES)
    def _(piece):
        @pl.loop(0, bands // PIECES, unroll=4)
        def _(j):
            band = piece * (bands // PIECES) + j
            block = block_ref[band]
            for part in range(2):
                outgoing[2 * band + part] = source[block, :, part * width : (part + 1) * width]

        leave(piece).start()

    state[...] = dot(hidden[0], out_w[:, :full]) + dot(hidden[1], out_o[:, :full])
    keep[...] = (mine.astype(F32) + state[:, half(core, width)]).astype(BF16)
    send[...] = (theirs.astype(F32) + state[:, half(1 - core, width)]).astype(BF16)
    for piece in range(PIECES):
        leave(piece).wait()


def mesh_update(arrived, owner_block, core, mesh, mesh_other, weights, blocks):
    pieces, rows, width = arrived.shape
    flat = jax.ShapeDtypeStruct(mesh.shape, BF16)
    leaving = arrived.shape
    dma = pltpu.SemaphoreType.DMA
    return pl.pallas_call(
        mesh_body,
        out_shape=(flat, flat, pltpu.HBM(leaving, BF16)),
        grid_spec=pltpu.PrefetchScalarGridSpec(
            num_scalar_prefetch=2,
            in_specs=[hbm()] + [vmem()] * 8,
            out_specs=[vmem(), vmem(), hbm()],
            scratch_shapes=[
                pltpu.VMEM(arrived.shape, BF16),
                pltpu.VMEM((blocks, rows, 2 * width), F32),
                pltpu.VMEM((blocks * rows, 2 * width), F32),
                pltpu.VMEM((blocks, rows, 2 * width), BF16),
                pltpu.VMEM(leaving, BF16),
                dma((PIECES,)),
                dma((PIECES,)),
            ],
        ),
        compiler_params=NARROW,
        cost_estimate=pl.CostEstimate(flops=10**9, bytes_accessed=12 * MB, transcendentals=1 << 17),
        name="mesh_update",
    )(owner_block, core, *stay(arrived), mesh, mesh_other, *weights)


def decode_body(
    slot_ref, target_ref, picked_hbm, start, tiles_hbm, out_hbm,
    picked, tiles, acc, out, picked_sem, tiles_sem, out_sem,
):
    count = tiles.shape[0]
    blocks = acc.shape[0]
    picked_start, picked_ready = fetch(picked_hbm, picked, picked_sem, PIECES)
    tiles_start, tiles_ready = fetch(tiles_hbm, tiles, tiles_sem, PIECES)
    per = blocks // PIECES
    for piece in range(PIECES):
        picked_start(piece)
    tiles_start(0)

    @pl.loop(0, PIECES)
    def _(piece):
        @pl.loop(0, per, unroll=4)
        def _(j):
            acc[piece * per + j] = start[piece * per + j].astype(F32)

    for piece in range(PIECES):
        picked_ready(piece)
    for piece in range(1, PIECES):
        tiles_start(piece)

    @pl.loop(0, PIECES)
    def _(piece):
        tiles_ready(piece)

        @pl.loop(0, count // PIECES // UNROLL)
        def _(j):
            base = piece * (count // PIECES) + j * UNROLL
            for i in range(UNROLL):
                acc[target_ref[base + i]] += dot(tiles[base + i], picked[slot_ref[base + i]])

    def leave(k):
        at = pl.ds(k * per, per)
        return pltpu.make_async_copy(out.at[at], out_hbm.at[at], out_sem.at[k])

    @pl.loop(0, PIECES)
    def _(piece):
        @pl.loop(0, per, unroll=4)
        def _(j):
            out[piece * per + j] = acc[piece * per + j].astype(BF16)

        leave(piece).start()

    for piece in range(PIECES):
        leave(piece).wait()


def decode(picked, grid_blocks, tiles, slot, target):
    count, edge, _ = tiles.shape
    width = grid_blocks.shape[2]
    dma = pltpu.SemaphoreType.DMA
    return pl.pallas_call(
        decode_body,
        out_shape=jax.ShapeDtypeStruct(grid_blocks.shape, BF16),
        grid_spec=pltpu.PrefetchScalarGridSpec(
            num_scalar_prefetch=2,
            in_specs=[hbm(), vmem(), hbm()],
            out_specs=hbm(),
            scratch_shapes=[
                pltpu.VMEM(picked.shape, BF16),
                pltpu.VMEM(tiles.shape, BF16),
                pltpu.VMEM(grid_blocks.shape, F32),
                pltpu.VMEM(grid_blocks.shape, BF16),
                *[dma((PIECES,))] * 3,
            ],
        ),
        compiler_params=pltpu.CompilerParams(vmem_limit_bytes=40 * MB),
        cost_estimate=pl.CostEstimate(
            flops=2 * count * edge * edge * width, bytes_accessed=16 * MB, transcendentals=0
        ),
        name="decode",
    )(slot, target, *stay(picked), grid_blocks, *stay(tiles))


def swap(x):
    return lax.ppermute(x, "mp", SWAP)


def owner_blocks(row):
    bands = lax.axis_size("band")
    me = lax.axis_index("band")
    table = row
    bit = 1
    while bit < bands:
        table = jnp.concatenate([table, lax.ppermute(table, "band", [(k, k ^ bit) for k in range(bands)])])
        bit *= 2
    number = jnp.arange(bands, dtype=jnp.int32)
    column = jnp.sum(jnp.where(number[None, :] == me, table, 0), axis=1)
    moved = (number[:, None] ^ me) == number[None, :]
    return jnp.sum(jnp.where(moved, column[None, :], 0), axis=1).astype(jnp.int32)


def per_device(
    grid_nodes,
    mesh_nodes,
    send_weight,
    self_weight,
    pooled_weight,
    out_weight,
    encode_source,
    encode_slot,
    encode_tiles,
    slot_block,
    decode_slot,
    decode_target,
    decode_tiles,
):
    bands = lax.axis_size("band")
    core = lax.axis_index("mp").astype(jnp.int32)
    core_1 = core.reshape(1)
    edge = encode_tiles.shape[1]
    width = grid_nodes.shape[1]
    mesh_blocks = mesh_nodes.shape[0] // edge
    rows = edge // 2

    grid_other = swap(grid_nodes)
    halves = mesh_nodes.reshape(mesh_blocks, 2, rows, width)
    mesh_keep = lax.dynamic_index_in_dim(halves, core, 1, keepdims=False).reshape(-1, width)
    mesh_send = lax.dynamic_index_in_dim(halves, 1 - core, 1, keepdims=False).reshape(-1, width)
    out_flat = out_weight.reshape(out_weight.shape[0], -1)
    mesh_other = swap(mesh_send)
    self_other, pooled_other, out_other = swap(self_weight), swap(pooled_weight), swap(out_flat)

    own, near_weight, near_tiles = load("load_encode", (grid_nodes, send_weight, encode_tiles))
    slot_sums = encode(
        own, grid_other, near_weight, near_tiles, encode_source, encode_slot, core_1, bands
    )
    arrived = lax.all_to_all(slot_sums, ("band", "mp"), split_axis=0, concat_axis=0, tiled=True)
    keep, send, outgoing = mesh_update(
        arrived,
        owner_blocks(slot_block),
        core_1,
        mesh_keep,
        mesh_other,
        (self_weight, self_other, pooled_weight, pooled_other, out_flat, out_other),
        mesh_blocks,
    )
    returned = lax.all_to_all(outgoing, ("band", "mp"), split_axis=0, concat_axis=0, tiled=True)
    came = swap(send)
    came = came.reshape(mesh_blocks, 1, rows, width)
    kept = keep.reshape(mesh_blocks, 1, rows, width)
    mesh_state = jnp.concatenate(
        [jnp.where(core == 0, kept, came), jnp.where(core == 0, came, kept)], axis=1
    ).reshape(mesh_nodes.shape)
    grid_state = decode(
        returned.reshape(bands, edge, width),
        grid_nodes.reshape(-1, edge, width),
        decode_tiles,
        decode_slot,
        decode_target,
    )
    return grid_state.reshape(grid_nodes.shape), mesh_state


def solution(mesh):
    return jax.shard_map(
        per_device,
        mesh=mesh,
        in_specs=(
            P("band", "mp"),
            P("band", "mp"),
            P(None, "mp"),
            P(None, "mp"),
            P(None, "mp"),
            P("mp", None, None),
            P("band"),
            P("band"),
            P("band", None, None),
            P("band", None),
            P("band"),
            P("band"),
            P("band", None, None),
        ),
        out_specs=(P("band", "mp"), P("band", "mp")),
        check_vma=False,
    )
```

```python
import functools

import jax
import jax.numpy as jnp
from jax import lax
from jax.experimental import pallas as pl
from jax.experimental.pallas import tpu as pltpu
from jax.sharding import PartitionSpec as P

MB = 1 << 20
F32 = jnp.float32
BF16 = jnp.bfloat16
SWAP = [(0, 1), (1, 0)]


def silu(v):
    return v / (1.0 + jnp.exp(-v))


def dot(a, b):
    return jnp.dot(a, b, preferred_element_type=F32)


def half(i, width):
    return pl.ds(pl.multiple_of(i * width, width), width)


def fetch(source, target, semaphores, count):
    size = source.shape[0] // count

    def piece(k):
        rows = pl.ds(k * size, size)
        return pltpu.make_async_copy(source.at[rows], target.at[rows], semaphores.at[k])

    return lambda k: piece(k).start(), lambda k: piece(k).wait()


def hbm():
    return pl.BlockSpec(memory_space=pltpu.HBM)


def stay(*arrays):
    return tuple(pltpu.with_memory_space_constraint(a, pltpu.HBM) for a in arrays)


def vmem():
    return pl.BlockSpec(memory_space=pltpu.VMEM)


NARROW = pltpu.CompilerParams(vmem_limit_bytes=44 * MB)


def load_body(*refs):
    semaphores, sums, refs = refs[-1], refs[-2], refs[:-2]
    sources, targets = refs[: len(refs) // 2], refs[len(refs) // 2 :]
    copies = [pltpu.make_async_copy(x, y, semaphores.at[k]) for k, (x, y) in enumerate(zip(sources, targets))]
    for copy in copies:
        copy.start()

    @pl.loop(0, sums.shape[0], unroll=4)
    def _(k):
        sums[k] = jnp.zeros(sums.shape[1:], F32)

    for copy in copies:
        copy.wait()


def load(arrays, sums):
    count = len(arrays)
    return pl.pallas_call(
        load_body,
        out_shape=(*[pltpu.VMEM(a.shape, a.dtype) for a in arrays], pltpu.VMEM(sums, F32)),
        in_specs=[hbm()] * count,
        out_specs=tuple(vmem() for _ in range(count + 1)),
        scratch_shapes=[pltpu.SemaphoreType.DMA((count,))],
        compiler_params=pltpu.CompilerParams(vmem_limit_bytes=32 * MB),
        cost_estimate=pl.CostEstimate(flops=0, bytes_accessed=16 * MB, transcendentals=0),
        name="load_encode",
    )(*stay(*arrays))


PIECES = 4
TAG = 8


def encode_body(
    slot_ref, source_ref, link_ref, core_ref, own, other, weight, tiles, _, out_hbm, acc, message, out, out_sem,
):
    core = core_ref[0]
    blocks, edge, width = message.shape
    slots = acc.shape[0]
    count = tiles.shape[0]
    rows = edge // 2
    lanes = out.shape[2]
    many = blocks // 2
    inner = many * edge

    @pl.loop(0, 2)
    def _(step):
        at = pl.ds(pl.multiple_of(step * inner, inner), inner)
        z = dot(own[at, :], weight[half(core, width), :]) + dot(other[at, :], weight[half(1 - core, width), :])
        message[pl.ds(step * many, many)] = silu(z).astype(BF16).reshape(many, edge, width)

    for i in range(count):
        acc[slot_ref[i]] += dot(tiles[i], message[source_ref[i]])

    size = 2 * slots // PIECES

    def leave(k):
        at = pl.ds(k * size, size)
        return pltpu.make_async_copy(out.at[at], out_hbm.at[at], out_sem.at[k])

    @pl.loop(0, PIECES)
    def _(piece):
        @pl.loop(0, slots // PIECES, unroll=4)
        def _(j):
            slot = piece * (slots // PIECES) + j
            tag = jnp.full((TAG, lanes), link_ref[slot].astype(F32), F32).astype(BF16)
            for part in range(2):
                value = acc[slot, part * rows : (part + 1) * rows, :].astype(BF16)
                for column in range(2):
                    out[2 * slot + part, column * rows : (column + 1) * rows, :] = value[
                        :, column * lanes : (column + 1) * lanes
                    ]
                out[2 * slot + part, 2 * rows :, :] = tag

        leave(piece).start()

    for piece in range(PIECES):
        leave(piece).wait()


def encode(own, other, weight, tiles, sums, source, slot, link, core, slots):
    count, edge, _ = tiles.shape
    width = weight.shape[1]
    sent = (2 * slots, edge + TAG, width // 2)
    dma = pltpu.SemaphoreType.DMA
    return pl.pallas_call(
        encode_body,
        out_shape=(pltpu.HBM(sent, BF16), pltpu.VMEM(sums.shape, F32)),
        input_output_aliases={8: 1},
        grid_spec=pltpu.PrefetchScalarGridSpec(
            num_scalar_prefetch=4,
            in_specs=[vmem()] * 5,
            out_specs=(hbm(), vmem()),
            scratch_shapes=[
                pltpu.VMEM((own.shape[0] // edge, edge, width), BF16),
                pltpu.VMEM(sent, BF16),
                dma((PIECES,)),
            ],
        ),
        compiler_params=pltpu.CompilerParams(vmem_limit_bytes=32 * MB),
        cost_estimate=pl.CostEstimate(
            flops=2 * count * edge * edge * width, bytes_accessed=16 * MB, transcendentals=own.shape[0] * width
        ),
        name="encode",
    )(slot, source, link, core, own, other, weight, tiles, sums)[0]


def mesh_body(
    core_ref, arrived_hbm, mine_ref, theirs_ref, self_w, self_o, pool_w, pool_o, out_w, out_o, keep, send,
    outgoing_hbm, arrived, acc, state, source, outgoing, block_ref, arrived_sem, out_sem,
):
    core = core_ref[0]
    bands = arrived.shape[0] // 2
    lanes = arrived.shape[2]
    rows = acc.shape[1]
    width = 2 * lanes
    arrived_start, ready = fetch(arrived_hbm, arrived, arrived_sem, PIECES)
    for piece in range(PIECES):
        arrived_start(piece)
    acc[...] = jnp.zeros(acc.shape, F32)

    @pl.loop(0, PIECES)
    def _(piece):
        ready(piece)

        @pl.loop(0, bands // PIECES, unroll=16)
        def _(j):
            band = piece * (bands // PIECES) + j
            tag = arrived[2 * band, 2 * rows :, :].astype(F32)
            block = jnp.max(tag).astype(jnp.int32)
            block_ref[band] = block

        @pl.loop(0, bands // PIECES, unroll=2)
        def _(j):
            band = piece * (bands // PIECES) + j
            block = block_ref[band]
            for part in range(2):
                for column in range(2):
                    at = (2 * part + column) * lanes
                    acc[block, :, at : at + lanes] += arrived[
                        2 * band + part, column * rows : (column + 1) * rows, :
                    ].astype(F32)

    pooled = acc[...].reshape(-1, 2 * width).astype(BF16)
    mine, theirs = mine_ref[...], theirs_ref[...]
    hidden = []
    for sw, pw in ((self_w, pool_w), (self_o, pool_o)):
        inner = (
            dot(mine, sw[half(core, width), :]) + dot(theirs, sw[half(1 - core, width), :]) + dot(pooled, pw[...])
        )
        hidden.append(silu(inner).astype(BF16))
    full = 2 * width
    sent = dot(hidden[0], out_w[:, full:]) + dot(hidden[1], out_o[:, full:])
    source[...] = sent.astype(BF16).reshape(source.shape)

    size = 2 * bands // PIECES

    def leave(k):
        at = pl.ds(k * size, size)
        return pltpu.make_async_copy(outgoing.at[at], outgoing_hbm.at[at], out_sem.at[k])

    @pl.loop(0, PIECES)
    def _(piece):
        @pl.loop(0, bands // PIECES, unroll=4)
        def _(j):
            band = piece * (bands // PIECES) + j
            block = block_ref[band]
            for part in range(2):
                outgoing[2 * band + part] = source[block, :, part * width : (part + 1) * width]

        leave(piece).start()

    state[...] = dot(hidden[0], out_w[:, :full]) + dot(hidden[1], out_o[:, :full])
    keep[...] = (mine.astype(F32) + state[:, half(core, width)]).astype(BF16)
    send[...] = (theirs.astype(F32) + state[:, half(1 - core, width)]).astype(BF16)
    for piece in range(PIECES):
        leave(piece).wait()


def mesh_update(arrived, core, mesh, mesh_other, weights, blocks):
    pieces, height, lanes = arrived.shape
    rows, width = (height - TAG) // 2, 2 * lanes
    flat = jax.ShapeDtypeStruct(mesh.shape, BF16)
    leaving = (pieces, rows, width)
    dma = pltpu.SemaphoreType.DMA
    return pl.pallas_call(
        mesh_body,
        out_shape=(flat, flat, pltpu.HBM(leaving, BF16)),
        grid_spec=pltpu.PrefetchScalarGridSpec(
            num_scalar_prefetch=1,
            in_specs=[hbm()] + [vmem()] * 8,
            out_specs=[vmem(), vmem(), hbm()],
            scratch_shapes=[
                pltpu.VMEM(arrived.shape, BF16),
                pltpu.VMEM((blocks, rows, 2 * width), F32),
                pltpu.VMEM((blocks * rows, 2 * width), F32),
                pltpu.VMEM((blocks, rows, 2 * width), BF16),
                pltpu.VMEM(leaving, BF16),
                pltpu.SMEM((pieces // 2,), jnp.int32),
                dma((PIECES,)),
                dma((PIECES,)),
            ],
        ),
        compiler_params=NARROW,
        cost_estimate=pl.CostEstimate(flops=10**9, bytes_accessed=12 * MB, transcendentals=1 << 17),
        name="mesh_update",
    )(core, *stay(arrived), mesh, mesh_other, *weights)


def decode_body(
    slot_ref, target_ref, picked_hbm, start, tiles_hbm, out_hbm,
    picked, tiles, acc, out, picked_sem, tiles_sem, out_sem,
):
    count = tiles.shape[0]
    blocks = acc.shape[0]
    picked_start, picked_ready = fetch(picked_hbm, picked, picked_sem, PIECES)
    ends = [0, count // 4, count * 5 // 8, count]

    def bring(k):
        at = pl.ds(ends[k], ends[k + 1] - ends[k])
        return pltpu.make_async_copy(tiles_hbm.at[at], tiles.at[at], tiles_sem.at[k])

    per = blocks // PIECES
    for piece in range(PIECES):
        picked_start(piece)
    bring(0).start()

    @pl.loop(0, PIECES)
    def _(piece):
        @pl.loop(0, per, unroll=4)
        def _(j):
            acc[piece * per + j] = start[piece * per + j].astype(F32)

    for piece in range(PIECES):
        picked_ready(piece)
    for k in range(1, 3):
        bring(k).start()
    for k in range(3):
        bring(k).wait()
        for i in range(ends[k], ends[k + 1]):
            acc[target_ref[i]] += dot(tiles[i], picked[slot_ref[i]])

    def leave(k):
        at = pl.ds(k * per, per)
        return pltpu.make_async_copy(out.at[at], out_hbm.at[at], out_sem.at[k])

    @pl.loop(0, PIECES)
    def _(piece):
        @pl.loop(0, per, unroll=4)
        def _(j):
            out[piece * per + j] = acc[piece * per + j].astype(BF16)

        leave(piece).start()

    for piece in range(PIECES):
        leave(piece).wait()


def decode(picked, grid_blocks, tiles, slot, target):
    count, edge, _ = tiles.shape
    width = grid_blocks.shape[2]
    dma = pltpu.SemaphoreType.DMA
    return pl.pallas_call(
        decode_body,
        out_shape=jax.ShapeDtypeStruct(grid_blocks.shape, BF16),
        grid_spec=pltpu.PrefetchScalarGridSpec(
            num_scalar_prefetch=2,
            in_specs=[hbm(), vmem(), hbm()],
            out_specs=hbm(),
            scratch_shapes=[
                pltpu.VMEM(picked.shape, BF16),
                pltpu.VMEM(tiles.shape, BF16),
                pltpu.VMEM(grid_blocks.shape, F32),
                pltpu.VMEM(grid_blocks.shape, BF16),
                *[dma((PIECES,))] * 3,
            ],
        ),
        compiler_params=pltpu.CompilerParams(vmem_limit_bytes=40 * MB),
        cost_estimate=pl.CostEstimate(
            flops=2 * count * edge * edge * width, bytes_accessed=16 * MB, transcendentals=0
        ),
        name="decode",
    )(slot, target, *stay(picked), grid_blocks, *stay(tiles))


def swap(x):
    return lax.ppermute(x, "mp", SWAP)


def per_device(
    grid_nodes,
    mesh_nodes,
    send_weight,
    self_weight,
    pooled_weight,
    out_weight,
    encode_source,
    encode_slot,
    encode_tiles,
    slot_block,
    decode_slot,
    decode_target,
    decode_tiles,
):
    bands = lax.axis_size("band")
    core = lax.axis_index("mp").astype(jnp.int32)
    core_1 = core.reshape(1)
    edge = encode_tiles.shape[1]
    width = grid_nodes.shape[1]
    mesh_blocks = mesh_nodes.shape[0] // edge
    rows = edge // 2

    grid_other = swap(grid_nodes)
    halves = mesh_nodes.reshape(mesh_blocks, 2, rows, width)
    mesh_keep = lax.dynamic_index_in_dim(halves, core, 1, keepdims=False).reshape(-1, width)
    mesh_send = lax.dynamic_index_in_dim(halves, 1 - core, 1, keepdims=False).reshape(-1, width)
    out_flat = out_weight.reshape(out_weight.shape[0], -1)
    mesh_other = swap(mesh_send)
    self_other, pooled_other, out_other = swap(self_weight), swap(pooled_weight), swap(out_flat)

    own, near_weight, near_tiles, sums = load((grid_nodes, send_weight, encode_tiles), (bands, edge, width))
    slot_sums = encode(
        own, grid_other, near_weight, near_tiles, sums, encode_source, encode_slot, slot_block[0], core_1, bands
    )
    arrived = lax.all_to_all(slot_sums, ("band", "mp"), split_axis=0, concat_axis=0, tiled=True)
    keep, send, outgoing = mesh_update(
        arrived,
        core_1,
        mesh_keep,
        mesh_other,
        (self_weight, self_other, pooled_weight, pooled_other, out_flat, out_other),
        mesh_blocks,
    )
    returned = lax.all_to_all(outgoing, ("band", "mp"), split_axis=0, concat_axis=0, tiled=True)
    came = swap(send)
    came = came.reshape(mesh_blocks, 1, rows, width)
    kept = keep.reshape(mesh_blocks, 1, rows, width)
    mesh_state = jnp.concatenate(
        [jnp.where(core == 0, kept, came), jnp.where(core == 0, came, kept)], axis=1
    ).reshape(mesh_nodes.shape)
    grid_state = decode(
        returned.reshape(bands, edge, width),
        grid_nodes.reshape(-1, edge, width),
        decode_tiles,
        decode_slot,
        decode_target,
    )
    return grid_state.reshape(grid_nodes.shape), mesh_state


def solution(mesh):
    return jax.shard_map(
        per_device,
        mesh=mesh,
        in_specs=(
            P("band", "mp"),
            P("band", "mp"),
            P(None, "mp"),
            P(None, "mp"),
            P(None, "mp"),
            P("mp", None, None),
            P("band"),
            P("band"),
            P("band", None, None),
            P("band", None),
            P("band"),
            P("band"),
            P("band", None, None),
        ),
        out_specs=(P("band", "mp"), P("band", "mp")),
        check_vma=False,
    )
```

```python
import functools

import jax
import jax.numpy as jnp
from jax import lax
from jax.experimental import pallas as pl
from jax.experimental.pallas import tpu as pltpu
from jax.sharding import PartitionSpec as P

MB = 1 << 20
F32 = jnp.float32
BF16 = jnp.bfloat16
SWAP = [(0, 1), (1, 0)]


def silu(v):
    return v / (1.0 + jnp.exp(-v))


def dot(a, b):
    return jnp.dot(a, b, preferred_element_type=F32)


def half(i, width):
    return pl.ds(pl.multiple_of(i * width, width), width)


def fetch(source, target, semaphores, count):
    size = source.shape[0] // count

    def piece(k):
        rows = pl.ds(k * size, size)
        return pltpu.make_async_copy(source.at[rows], target.at[rows], semaphores.at[k])

    return lambda k: piece(k).start(), lambda k: piece(k).wait()


def hbm():
    return pl.BlockSpec(memory_space=pltpu.HBM)


def stay(*arrays):
    return tuple(pltpu.with_memory_space_constraint(a, pltpu.HBM) for a in arrays)


def vmem():
    return pl.BlockSpec(memory_space=pltpu.VMEM)


NARROW = pltpu.CompilerParams(vmem_limit_bytes=44 * MB)


def load_body(*refs):
    semaphores, sums, refs = refs[-1], refs[-2], refs[:-2]
    sources, targets = refs[: len(refs) // 2], refs[len(refs) // 2 :]
    copies = [pltpu.make_async_copy(x, y, semaphores.at[k]) for k, (x, y) in enumerate(zip(sources, targets))]
    for copy in copies:
        copy.start()

    @pl.loop(0, sums.shape[0], unroll=4)
    def _(k):
        sums[k] = jnp.zeros(sums.shape[1:], F32)

    for copy in copies:
        copy.wait()


def load(arrays, sums):
    count = len(arrays)
    return pl.pallas_call(
        load_body,
        out_shape=(*[pltpu.VMEM(a.shape, a.dtype) for a in arrays], pltpu.VMEM(sums, F32)),
        in_specs=[hbm()] * count,
        out_specs=tuple(vmem() for _ in range(count + 1)),
        scratch_shapes=[pltpu.SemaphoreType.DMA((count,))],
        compiler_params=pltpu.CompilerParams(vmem_limit_bytes=32 * MB),
        cost_estimate=pl.CostEstimate(flops=0, bytes_accessed=16 * MB, transcendentals=0),
        name="load_encode",
    )(*stay(*arrays))


PIECES = 4
TAG = 8


def encode_body(
    slot_ref, source_ref, link_ref, core_ref, own, other, weight, tiles, _, out_hbm, acc, message, out, out_sem,
):
    core = core_ref[0]
    blocks, edge, width = message.shape
    slots = acc.shape[0]
    count = tiles.shape[0]
    rows = edge // 2
    lanes = out.shape[2]
    z = dot(own[...], weight[half(core, width), :]) + dot(other[...], weight[half(1 - core, width), :])
    message[...] = silu(z).astype(BF16).reshape(blocks, edge, width)

    for i in range(count):
        acc[slot_ref[i]] += dot(tiles[i], message[source_ref[i]])

    size = 2 * slots // PIECES

    def leave(k):
        at = pl.ds(k * size, size)
        return pltpu.make_async_copy(out.at[at], out_hbm.at[at], out_sem.at[k])

    @pl.loop(0, PIECES)
    def _(piece):
        @pl.loop(0, slots // PIECES, unroll=4)
        def _(j):
            slot = piece * (slots // PIECES) + j
            tag = jnp.full((TAG, lanes), link_ref[slot].astype(F32), F32).astype(BF16)
            for part in range(2):
                value = acc[slot, part * rows : (part + 1) * rows, :].astype(BF16)
                for column in range(2):
                    out[2 * slot + part, column * rows : (column + 1) * rows, :] = value[
                        :, column * lanes : (column + 1) * lanes
                    ]
                out[2 * slot + part, 2 * rows :, :] = tag

        leave(piece).start()

    for piece in range(PIECES):
        leave(piece).wait()


def encode(own, other, weight, tiles, sums, source, slot, link, core, slots):
    count, edge, _ = tiles.shape
    width = weight.shape[1]
    sent = (2 * slots, edge + TAG, width // 2)
    dma = pltpu.SemaphoreType.DMA
    return pl.pallas_call(
        encode_body,
        out_shape=(pltpu.HBM(sent, BF16), pltpu.VMEM(sums.shape, F32)),
        input_output_aliases={8: 1},
        grid_spec=pltpu.PrefetchScalarGridSpec(
            num_scalar_prefetch=4,
            in_specs=[vmem()] * 5,
            out_specs=(hbm(), vmem()),
            scratch_shapes=[
                pltpu.VMEM((own.shape[0] // edge, edge, width), BF16),
                pltpu.VMEM(sent, BF16),
                dma((PIECES,)),
            ],
        ),
        compiler_params=pltpu.CompilerParams(vmem_limit_bytes=32 * MB),
        cost_estimate=pl.CostEstimate(
            flops=2 * count * edge * edge * width, bytes_accessed=16 * MB, transcendentals=own.shape[0] * width
        ),
        name="encode",
    )(slot, source, link, core, own, other, weight, tiles, sums)[0]


def mesh_body(
    core_ref, arrived_hbm, mine_ref, theirs_ref, self_w, self_o, pool_w, pool_o, out_w, out_o, keep, send,
    outgoing_hbm, arrived, acc, state, source, outgoing, block_ref, arrived_sem, out_sem,
):
    core = core_ref[0]
    bands = arrived.shape[0] // 2
    lanes = arrived.shape[2]
    rows = acc.shape[1]
    width = 2 * lanes
    arrived_start, ready = fetch(arrived_hbm, arrived, arrived_sem, PIECES)
    for piece in range(PIECES):
        arrived_start(piece)
    acc[...] = jnp.zeros(acc.shape, F32)

    @pl.loop(0, PIECES)
    def _(piece):
        ready(piece)

        @pl.loop(0, bands // PIECES, unroll=16)
        def _(j):
            band = piece * (bands // PIECES) + j
            tag = arrived[2 * band, 2 * rows :, :].astype(F32)
            block = jnp.max(tag).astype(jnp.int32)
            block_ref[band] = block

        @pl.loop(0, bands // PIECES, unroll=2)
        def _(j):
            band = piece * (bands // PIECES) + j
            block = block_ref[band]
            for part in range(2):
                for column in range(2):
                    at = (2 * part + column) * lanes
                    acc[block, :, at : at + lanes] += arrived[
                        2 * band + part, column * rows : (column + 1) * rows, :
                    ].astype(F32)

    pooled = acc[...].reshape(-1, 2 * width).astype(BF16)
    mine, theirs = mine_ref[...], theirs_ref[...]
    hidden = []
    for sw, pw in ((self_w, pool_w), (self_o, pool_o)):
        inner = (
            dot(mine, sw[half(core, width), :]) + dot(theirs, sw[half(1 - core, width), :]) + dot(pooled, pw[...])
        )
        hidden.append(silu(inner).astype(BF16))
    full = 2 * width
    sent = dot(hidden[0], out_w[:, full:]) + dot(hidden[1], out_o[:, full:])
    source[...] = sent.astype(BF16).reshape(source.shape)

    size = 2 * bands // PIECES

    def leave(k):
        at = pl.ds(k * size, size)
        return pltpu.make_async_copy(outgoing.at[at], outgoing_hbm.at[at], out_sem.at[k])

    @pl.loop(0, PIECES)
    def _(piece):
        @pl.loop(0, bands // PIECES, unroll=4)
        def _(j):
            band = piece * (bands // PIECES) + j
            block = block_ref[band]
            for part in range(2):
                outgoing[2 * band + part] = source[block, :, part * width : (part + 1) * width]

        leave(piece).start()

    state[...] = dot(hidden[0], out_w[:, :full]) + dot(hidden[1], out_o[:, :full])
    keep[...] = (mine.astype(F32) + state[:, half(core, width)]).astype(BF16)
    send[...] = (theirs.astype(F32) + state[:, half(1 - core, width)]).astype(BF16)
    for piece in range(PIECES):
        leave(piece).wait()


def mesh_update(arrived, core, mesh, mesh_other, weights, blocks):
    pieces, height, lanes = arrived.shape
    rows, width = (height - TAG) // 2, 2 * lanes
    flat = jax.ShapeDtypeStruct(mesh.shape, BF16)
    leaving = (pieces, rows, width)
    dma = pltpu.SemaphoreType.DMA
    return pl.pallas_call(
        mesh_body,
        out_shape=(flat, flat, pltpu.HBM(leaving, BF16)),
        grid_spec=pltpu.PrefetchScalarGridSpec(
            num_scalar_prefetch=1,
            in_specs=[hbm()] + [vmem()] * 8,
            out_specs=[vmem(), vmem(), hbm()],
            scratch_shapes=[
                pltpu.VMEM(arrived.shape, BF16),
                pltpu.VMEM((blocks, rows, 2 * width), F32),
                pltpu.VMEM((blocks * rows, 2 * width), F32),
                pltpu.VMEM((blocks, rows, 2 * width), BF16),
                pltpu.VMEM(leaving, BF16),
                pltpu.SMEM((pieces // 2,), jnp.int32),
                dma((PIECES,)),
                dma((PIECES,)),
            ],
        ),
        compiler_params=NARROW,
        cost_estimate=pl.CostEstimate(flops=10**9, bytes_accessed=12 * MB, transcendentals=1 << 17),
        name="mesh_update",
    )(core, *stay(arrived), mesh, mesh_other, *weights)


def decode_body(
    slot_ref, target_ref, picked_hbm, start, tiles_hbm, out_hbm,
    picked, tiles, acc, out, picked_sem, tiles_sem, out_sem,
):
    count = tiles.shape[0]
    blocks = acc.shape[0]
    picked_start, picked_ready = fetch(picked_hbm, picked, picked_sem, PIECES)
    ends = [0, count // 4, count * 5 // 8, count]

    def bring(k):
        at = pl.ds(ends[k], ends[k + 1] - ends[k])
        return pltpu.make_async_copy(tiles_hbm.at[at], tiles.at[at], tiles_sem.at[k])

    per = blocks // PIECES
    for piece in range(PIECES):
        picked_start(piece)
    bring(0).start()

    @pl.loop(0, PIECES)
    def _(piece):
        @pl.loop(0, per, unroll=4)
        def _(j):
            acc[piece * per + j] = start[piece * per + j].astype(F32)

    for piece in range(PIECES):
        picked_ready(piece)
    for k in range(1, 3):
        bring(k).start()
    for k in range(3):
        bring(k).wait()
        for i in range(ends[k], ends[k + 1]):
            acc[target_ref[i]] += dot(tiles[i], picked[slot_ref[i]])

    def leave(k):
        at = pl.ds(k * per, per)
        return pltpu.make_async_copy(out.at[at], out_hbm.at[at], out_sem.at[k])

    @pl.loop(0, PIECES)
    def _(piece):
        @pl.loop(0, per, unroll=4)
        def _(j):
            out[piece * per + j] = acc[piece * per + j].astype(BF16)

        leave(piece).start()

    for piece in range(PIECES):
        leave(piece).wait()


def decode(picked, grid_blocks, tiles, slot, target):
    count, edge, _ = tiles.shape
    width = grid_blocks.shape[2]
    dma = pltpu.SemaphoreType.DMA
    return pl.pallas_call(
        decode_body,
        out_shape=jax.ShapeDtypeStruct(grid_blocks.shape, BF16),
        grid_spec=pltpu.PrefetchScalarGridSpec(
            num_scalar_prefetch=2,
            in_specs=[hbm(), vmem(), hbm()],
            out_specs=hbm(),
            scratch_shapes=[
                pltpu.VMEM(picked.shape, BF16),
                pltpu.VMEM(tiles.shape, BF16),
                pltpu.VMEM(grid_blocks.shape, F32),
                pltpu.VMEM(grid_blocks.shape, BF16),
                *[dma((PIECES,))] * 3,
            ],
        ),
        compiler_params=pltpu.CompilerParams(vmem_limit_bytes=40 * MB),
        cost_estimate=pl.CostEstimate(
            flops=2 * count * edge * edge * width, bytes_accessed=16 * MB, transcendentals=0
        ),
        name="decode",
    )(slot, target, *stay(picked), grid_blocks, *stay(tiles))


def swap(x):
    return lax.ppermute(x, "mp", SWAP)


def per_device(
    grid_nodes,
    mesh_nodes,
    send_weight,
    self_weight,
    pooled_weight,
    out_weight,
    encode_source,
    encode_slot,
    encode_tiles,
    slot_block,
    decode_slot,
    decode_target,
    decode_tiles,
):
    bands = lax.axis_size("band")
    core = lax.axis_index("mp").astype(jnp.int32)
    core_1 = core.reshape(1)
    edge = encode_tiles.shape[1]
    width = grid_nodes.shape[1]
    mesh_blocks = mesh_nodes.shape[0] // edge
    rows = edge // 2

    grid_other = swap(grid_nodes)
    halves = mesh_nodes.reshape(mesh_blocks, 2, rows, width)
    mesh_keep = lax.dynamic_index_in_dim(halves, core, 1, keepdims=False).reshape(-1, width)
    mesh_send = lax.dynamic_index_in_dim(halves, 1 - core, 1, keepdims=False).reshape(-1, width)
    out_flat = out_weight.reshape(out_weight.shape[0], -1)
    mesh_other = swap(mesh_send)
    self_other, pooled_other, out_other = swap(self_weight), swap(pooled_weight), swap(out_flat)

    own, near_weight, near_tiles, sums = load((grid_nodes, send_weight, encode_tiles), (bands, edge, width))
    slot_sums = encode(
        own, grid_other, near_weight, near_tiles, sums, encode_source, encode_slot, slot_block[0], core_1, bands
    )
    arrived = lax.all_to_all(slot_sums, ("band", "mp"), split_axis=0, concat_axis=0, tiled=True)
    keep, send, outgoing = mesh_update(
        arrived,
        core_1,
        mesh_keep,
        mesh_other,
        (self_weight, self_other, pooled_weight, pooled_other, out_flat, out_other),
        mesh_blocks,
    )
    returned = lax.all_to_all(outgoing, ("band", "mp"), split_axis=0, concat_axis=0, tiled=True)
    came = swap(send)
    came = came.reshape(mesh_blocks, 1, rows, width)
    kept = keep.reshape(mesh_blocks, 1, rows, width)
    mesh_state = jnp.concatenate(
        [jnp.where(core == 0, kept, came), jnp.where(core == 0, came, kept)], axis=1
    ).reshape(mesh_nodes.shape)
    grid_state = decode(
        returned.reshape(bands, edge, width),
        grid_nodes.reshape(-1, edge, width),
        decode_tiles,
        decode_slot,
        decode_target,
    )
    return grid_state.reshape(grid_nodes.shape), mesh_state


def solution(mesh):
    return jax.shard_map(
        per_device,
        mesh=mesh,
        in_specs=(
            P("band", "mp"),
            P("band", "mp"),
            P(None, "mp"),
            P(None, "mp"),
            P(None, "mp"),
            P("mp", None, None),
            P("band"),
            P("band"),
            P("band", None, None),
            P("band", None),
            P("band"),
            P("band"),
            P("band", None, None),
        ),
        out_specs=(P("band", "mp"), P("band", "mp")),
        check_vma=False,
    )
```
